32 devices in a mesh: groups: 2 (over x), wide: 16 (over z, y, core).
Axes of the slice: x: 2, y: 2, z: 4, core: 2. Of those that a mesh axis runs over, the one named last changes fastest.
Arguments:
- embeddings: bfloat16 [65536, 768], P(('groups', 'wide')), parts along dimension 0, may hold values from -6 to 6
- row_owner: int32 [65536, 1], P(('groups', 'wide')), parts along dimension 0, may hold values from 0 to 15; in each aligned block of 2048 rows (0 to 2047, 2048 to 4095, ...) at most 256 rows name the same one
- row_cluster: int32 [65536], P(('groups', 'wide')), parts along dimension 0, may hold values from 0 to 7
Outputs:
- best_similarity: float32 [65536], P(('groups', 'wide')), parts along dimension 0
The draws below stay inside these ranges and needn't reach their ends.
There are 2 independent parts, one for each index of `groups`. The reference program is written for one: setup_inputs(seed, part) draws one part's arguments, and reference() takes and returns one part's arrays. A program takes and returns all parts, laid end to end along the dimension named above; each array names one. Nothing has to cross between parts.
Inputs may be any that keep to these rules, and one draw needn't show every extreme that they name: `row_owner`: among the rows of one device no owner is named more than 256 times, a bound that some block reaches.
All inputs are finite; a program needn't handle non-finite values.
Results may differ from the reference program's by a relative error of at most 0.0015.
Values may be sent and summed in bfloat16 or wider, within the bound.
A program may use at most 64 MiB of HBM per device.

```python
import math
import jax
import jax.numpy as jnp
import numpy as np
from jax import lax

D = 768
ROW_DEV = 2048
CL_DEV = 8
CAP = 256
ROWS = 32768
N_WIDE = 16


def with_ends(entries, own_key, smallest, top_value):
    longest = entries.shape.index(max(entries.shape))
    spots = []
    for shift in (0, 1):
        where = [jax.random.randint(jax.random.fold_in(own_key, axis), (), 0, length) for axis, length in enumerate(entries.shape)]
        where[longest] = (where[longest] + shift) % entries.shape[longest]
        spots.append(tuple(where))
    return entries.at[spots[0]].set(smallest).at[spots[1]].set(top_value)


def level_of(own_key, extent, shards, smallest, top_value):
    def one(dim, blocks):
        steps = jax.random.uniform(jax.random.fold_in(jax.random.fold_in(own_key, 6), dim), (blocks,), jnp.float32, smallest / len(shards), top_value / len(shards))
        return jnp.repeat(jnp.exp(steps), extent[dim] // blocks).reshape((-1,) + (1,) * (len(extent) - dim - 1))

    factor_of = one(*shards[0])
    for cut in shards[1:]:
        factor_of = factor_of * one(*cut)
    return factor_of


def cumulative_ranks(amount, lean):
    portions = [(1 << 20) // math.isqrt(rank ** lean) + 1 for rank in range(1, amount + 1)]
    scale = 1 + sum(portions) // (1 << 30)
    return np.cumsum(np.array([max(1, weight // scale) for weight in portions]))


def ranked_ids(own_key, dims, number_of, skew):
    grid = cumulative_ranks(number_of, skew)
    pick = jax.random.randint(jax.random.fold_in(own_key, 1), dims, 0, int(grid[number_of - 1]))
    grade = jnp.searchsorted(jnp.asarray(grid, jnp.int32), pick, side="right")
    return jax.random.permutation(jax.random.fold_in(own_key, 2), number_of)[grade].astype(jnp.int32)


def assign_block(stream_key, own, number, rows, number_of, top, reach, lean):
    order = jax.random.permutation(stream_key, number_of)
    crowded, usual = shares(number_of, rows * top, reach, lean, True), shares(number_of, rows * top, reach, lean, False)
    places = jnp.arange(number_of)

    def named(lengths, offset_by):
        used = int((lengths > 0).sum())
        fixed = max(1, used // 4)
        passed = fixed + (places - fixed + offset_by * (used - fixed)) % max(1, number_of - fixed)
        return jnp.zeros((number_of,), jnp.int32).at[order[jnp.where(places < fixed, places, passed)]].set(jnp.asarray(lengths, jnp.int32))

    lengths = jnp.where(number % 4 == 0, named(crowded, number // 4), named(usual, number - number // 4 - 1))
    mixed = jax.random.permutation(jax.random.fold_in(own, 3), number_of)
    giver, sink = mixed[0:number_of // 2 * 2:2], mixed[1:number_of // 2 * 2:2]
    slack = jnp.minimum(lengths[giver] - 1, reach - lengths[sink]) // 2
    slack = jnp.where((giver == order[0]) | (sink == order[0]) | (lengths[sink] == 0), 0, jnp.maximum(slack, 0))
    passed = jax.random.randint(jax.random.fold_in(own, 4), (number_of // 2,), 0, 1 << 20) % (slack + 1)
    lengths = lengths.at[giver].add(-passed).at[sink].add(passed)
    items = jnp.searchsorted(jnp.cumsum(lengths), jnp.arange(rows * top), side="right").astype(jnp.int32)
    grid = items.reshape(top, rows).T
    grid = grid[jax.random.permutation(jax.random.fold_in(own, 1), rows)]
    offset_by = jax.random.randint(jax.random.fold_in(own, 2), (rows, 1), 0, top)
    return jnp.take_along_axis(grid, (jnp.arange(top)[None, :] + offset_by) % top, axis=1)


def shares(amount, total, reach, lean, full):
    portions = [(1 << 20) // math.isqrt(standing ** lean) + 1 for standing in range(1, amount + 1)]
    largest = reach if full else min(reach, max(-(-total // amount), total * portions[0] // sum(portions)))
    least = 1 if total - largest >= amount - 1 else 0
    given, rest = [largest] + [least] * (amount - 1), total - largest - least * (amount - 1)
    while rest > 0:
        movable = [i for i in range(1, amount) if given[i] < largest] or [i for i in range(1, amount) if given[i] < reach]
        mass, remaining = sum([portions[i] for i in movable]), rest
        for i in movable:
            extra = min(reach - given[i], max(1, remaining * portions[i] // mass), rest)
            given[i] = given[i] + extra
            rest = rest - extra
    return np.array(given)


def scatter_about(rng, extent, scale, reach, cuts=(), held_as=jnp.bfloat16):
    entries = scale * jax.random.normal(rng, extent, jnp.float32)
    if cuts:
        entries = entries * level_of(rng, extent, cuts, -0.22, 0.18)
    return jnp.clip(entries, -reach, reach).astype(held_as)


def setup_inputs(seed: int = 0, part: int = 0) -> dict:
    seeds = jax.random.split(jax.random.key(seed), 4)
    part_keys = jax.random.split(jax.random.fold_in(seeds[3], part), 4)
    embeddings = scatter_about(part_keys[0], (ROWS, D), 1.0, 6.0, ((0, 16),))
    row_owner_keys = jax.random.split(jax.random.fold_in(part_keys[1], 1), ROWS // ROW_DEV)
    row_owner_turns = jax.random.permutation(jax.random.fold_in(part_keys[1], 3), ROWS // ROW_DEV)
    row_owner = jax.vmap(lambda own, number: assign_block(jax.random.fold_in(part_keys[1], 2), own, number, ROW_DEV, N_WIDE, 1, CAP, 2))(row_owner_keys, row_owner_turns).reshape((ROWS, 1))
    row_cluster = with_ends(ranked_ids(part_keys[2], (ROWS,), CL_DEV, 2), jax.random.fold_in(part_keys[2], 3), 0, CL_DEV - 1).astype(jnp.int32)
    return dict(embeddings=embeddings, row_owner=row_owner, row_cluster=row_cluster)


def reference(embeddings, row_owner, row_cluster):
    values = embeddings.astype(jnp.float32)
    scale = lax.rsqrt(lax.optimization_barrier(jnp.sum(values * values, axis=1, keepdims=True)) + 1e-06)
    unit = (values * scale).astype(jnp.bfloat16)
    owner = row_owner[:, 0].astype(jnp.int32)
    cluster = (owner * CL_DEV + row_cluster).astype(jnp.int32)
    order = jnp.argsort(cluster, stable=True).astype(jnp.int32)
    sorted_unit = unit[order]
    sorted_owner = owner[order]
    sorted_cluster = cluster[order]
    window = min(N_WIDE * CAP, ROWS)
    index = jnp.arange(window, dtype=jnp.int32)

    def visit(result, which):
        first = jnp.sum((owner < which).astype(jnp.int32)).astype(jnp.int32)
        start = jnp.minimum(first, ROWS - window).astype(jnp.int32)
        rows = lax.dynamic_slice_in_dim(sorted_unit, start, window, 0)
        keys = lax.dynamic_slice_in_dim(sorted_cluster, start, window, 0)
        owners = lax.dynamic_slice_in_dim(sorted_owner, start, window, 0)
        scores = jnp.dot(rows, rows.T, preferred_element_type=jnp.float32)
        mask = (keys[:, None] == keys[None, :]) & (index[:, None] != index[None, :])
        best = lax.optimization_barrier(jnp.max(jnp.where(mask, scores, jnp.float32(-1.0)), axis=1))
        current = lax.dynamic_slice_in_dim(result, start, window, 0)
        merged = jnp.where(owners == which, best, current)
        return (lax.dynamic_update_slice_in_dim(result, merged, start, 0), None)
    result, _ = lax.scan(visit, jnp.zeros((ROWS,), jnp.float32), jnp.arange(N_WIDE, dtype=jnp.int32))
    return jnp.zeros((ROWS,), jnp.float32).at[order].set(result)
```

```python
import functools

import jax
import jax.numpy as jnp
from jax import lax
from jax.experimental import pallas as pl
from jax.experimental.pallas import tpu as pltpu
from jax.sharding import PartitionSpec as P

WINDOW = 6
AHEAD = 3
BATCH = 4
STRIP = 256
LANES = 128


def fold_rows(tile):
    return jnp.max(tile.reshape(tile.shape[0] // 8, 8, tile.shape[1]), axis=0)


def spread(group, groups, block):
    return lax.rem(group + block, groups)


def sizes_of(rows, peers):
    cap = 2 * rows // peers
    far = (cap * 9 // 16 + 15) // 16 * 16
    near = (cap * 10 // 16 + 15) // 16 * 16
    first = far * 2 // 9 // 16 * 16
    return near, far, first


def bf16(x):
    return x.astype(jnp.float32).astype(jnp.bfloat16)


def dot(a, b, contract=((1,), (0,))):
    return lax.dot_general(a, b, (contract, ((), ())), preferred_element_type=jnp.float32)


def kernel(peers, groups, near, far, first, emb, owner, cluster, out, over,
           send, recv, id_col, id_row, row_best, col_best, ret_out, ret_in, of_kind, slots, high, low, table,
           low_edge, high_edge,
           count_out, count_in, counts, choices, chosen, over_out, over_in,
           first_send, first_recv, near_send, near_recv, far_send, far_recv, ret_send, ret_recv,
           count_send, count_recv, over_send, over_recv):
    me = lax.axis_index("wide")
    group = lax.axis_index("groups")
    rows = emb.shape[0]
    half = peers // 2
    rest = far - first
    near_at = half * first
    far_at = near_at + half * near
    total = far_at + half * rest
    kinds = counts.shape[1]

    def partner(block):
        hop = block // 2 + (block % 2) * half
        result, bit = 0, 1
        while bit < peers:
            result = result + bit * ((me // bit + hop // bit) % 2)
            bit *= 2
        return result

    def remote(src, dst, block, sends, recvs, at):
        return pltpu.make_async_remote_copy(
            src_ref=src, dst_ref=dst, send_sem=sends.at[at], recv_sem=recvs.at[at],
            device_id={"wide": partner(block)}, device_id_type=pl.DeviceIdType.MESH)

    def part(at, count):
        where = pl.ds(pl.multiple_of(at, 16), count)
        return send.at[where], recv.at[where]

    def first_copy(i):
        return remote(*part(i * first, first), 2 * i + 1, first_send, first_recv, i)

    def near_copy(i):
        return remote(*part(near_at + i * near, near), 2 * i, near_send, near_recv, i)

    def far_copy(i):
        return remote(*part(far_at + i * rest, rest), 2 * i + 1, far_send, far_recv, i)

    def answer(block):
        return remote(ret_out, ret_in.at[block], block, ret_send, ret_recv, block)

    def tell(block):
        return remote(count_out, count_in.at[block], block, count_send, count_recv, block)

    def warn(block):
        return pltpu.make_async_remote_copy(
            src_ref=over_out, dst_ref=over_in.at[block],
            send_sem=over_send.at[block], recv_sem=over_recv.at[block],
            device_id={"groups": spread(group, groups, block)},
            device_id_type=pl.DeviceIdType.MESH)

    barrier = pltpu.get_barrier_semaphore()

    @pl.loop(1, peers)
    def _(block):
        pl.semaphore_signal(
            barrier, inc=1, device_id={"wide": partner(block)},
            device_id_type=pl.DeviceIdType.MESH)

    @pl.loop(1, groups)
    def _(block):
        pl.semaphore_signal(
            barrier, inc=1, device_id={"groups": spread(group, groups, block)},
            device_id_type=pl.DeviceIdType.MESH)

    kind = owner[...] * (kinds // peers) + cluster[...]
    of_kind[...] = bf16(lax.broadcasted_iota(jnp.int32, (kinds, rows), 0) == kind)
    count_out[...] = dot(jnp.ones((8, rows), jnp.bfloat16), of_kind[...], ((1,), (1,)))
    upto = bf16(
        lax.broadcasted_iota(jnp.int32, (LANES, LANES), 0)
        <= lax.broadcasted_iota(jnp.int32, (LANES, LANES), 1))
    seen = jnp.zeros((kinds, 1), jnp.float32)
    ranks = []
    for start in range(0, rows, LANES):
        hot = of_kind[:, start:start + LANES]
        count = dot(hot, upto)
        ranks.append(jnp.sum(hot.astype(jnp.float32) * (count + seen), axis=0, keepdims=True) - 1.0)
        seen = seen + count[:, LANES - 1:LANES]
    rank = jnp.concatenate(ranks, axis=1)
    table[...] = jnp.zeros((LANES, LANES), jnp.float32)
    ret_out[...] = jnp.zeros(ret_out.shape, jnp.float32)
    row_best[...] = jnp.full(row_best.shape, -1.0, jnp.float32)

    pl.semaphore_wait(barrier, peers - 1 + groups - 1)

    @pl.loop(1, peers)
    def _(block):
        tell(block).start()

    count_in[0] = count_out[...]

    @pl.loop(1, peers)
    def _(block):
        tell(block).wait()

    for block in range(peers):
        counts[block:block + 1, :] = count_in[block][0:1, :]

    sizes = jnp.broadcast_to(jnp.sum(counts[...], axis=0, keepdims=True), (kinds, kinds))
    others = sizes.T
    before = (
        lax.broadcasted_iota(jnp.int32, (kinds, kinds), 0)
        < lax.broadcasted_iota(jnp.int32, (kinds, kinds), 1))
    above = (others > sizes) | ((others == sizes) & before)
    place = jnp.sum(above.astype(jnp.float32), axis=0, keepdims=True)
    sorter = bf16(
        lax.broadcasted_iota(jnp.int32, (kinds, kinds), 0) == place.astype(jnp.int32))

    def pack(key, count):
        hot = bf16(lax.broadcasted_iota(jnp.int32, (count, rows), 0) == key)
        picked = dot(hot, emb[...])
        scale = lax.rsqrt(jnp.sum(picked * picked, axis=1, keepdims=True) + 1e-06)
        return (picked * scale).astype(jnp.bfloat16)

    placed = dot(bf16(jnp.broadcast_to(place, (8, kinds))), of_kind[...])[0:1, :].astype(jnp.int32)
    hop = jnp.bitwise_xor(placed, me)
    early = (placed < peers) & (hop >= half) & (rank < first)
    key = jnp.where(early, (hop - half) * first + rank.astype(jnp.int32), -1)
    send[0:near_at] = pack(key, near_at)

    @pl.loop(0, half)
    def _(i):
        first_copy(i).start()

    hit = lax.broadcasted_iota(jnp.int32, (kinds, peers, kinds), 0) == place.astype(jnp.int32)[None]
    lines = bf16(jnp.where(hit, counts[...][None], 0.0))
    choices[...] = dot(
        lines.reshape(kinds * peers, kinds), jnp.ones((kinds, LANES), jnp.bfloat16)
    ).reshape(kinds, peers, LANES)
    lane = lax.broadcasted_iota(jnp.int32, (1, LANES), 1)
    tie = jnp.where(lane < peers, lane, 1 << 22).astype(jnp.float32)

    ranked = dot(bf16(counts[...]), sorter, ((1,), (1,)))
    chosen[0:peers, :] = (
        lax.broadcasted_iota(jnp.int32, (peers, LANES), 0)
        == lax.broadcasted_iota(jnp.int32, (peers, LANES), 1)).astype(jnp.float32)

    source = jnp.bitwise_xor(
        lax.broadcasted_iota(jnp.int32, (peers, kinds), 0) % 2, me // half)
    target = lax.broadcasted_iota(jnp.int32, (peers, kinds), 1)
    is_far = source != target // half
    filled = jnp.where((target < peers) & is_far, jnp.maximum(ranked, first), ranked)
    load = jnp.where(
        target < peers, jnp.where(is_far, filled, filled - (near - far)), 0.0)[:, :LANES]

    def choose(step, load):
        at = peers + step * BATCH
        more = [choices[at + i] for i in range(BATCH)]
        keys = [jnp.max(load + m, axis=0, keepdims=True) * LANES + tie for m in more]
        taken = jnp.zeros((1, LANES), jnp.float32)
        for i in range(BATCH):
            key = keys[i] + taken
            pick = key == jnp.min(key, axis=1, keepdims=True)
            chosen[pl.ds(at + i, 1), :] = pick.astype(jnp.float32)
            load = jnp.where(pick, load + more[i], load)
            taken = jnp.where(pick, 1 << 22, taken)
        return load

    load = lax.fori_loop(0, (kinds - peers) // BATCH, choose, load)
    most = jnp.max(jnp.max(load, axis=1, keepdims=True), axis=0, keepdims=True)
    over_out[...] = jnp.broadcast_to((most > far).astype(jnp.float32), (8, LANES))
    over_in[0] = over_out[...]

    @pl.loop(1, groups)
    def _(block):
        warn(block).start()

    picks = bf16(chosen[...])
    together = dot(picks, picks, ((1,), (1,)))
    begins = dot(bf16(filled), bf16(jnp.where(before, together, 0.0)))
    names = bf16(lax.broadcasted_iota(jnp.int32, (8, LANES), 1))
    by_place = dot(names, picks, ((1,), (1,)))
    mine = by_place[0:1, :].astype(jnp.int32) == me
    low_edge[...] = jnp.where(mine, begins, 0.0)
    high_edge[...] = jnp.where(mine, begins + ranked, 0.0)
    facts = jnp.where(
        lax.broadcasted_iota(jnp.int32, (8, kinds), 0) == 0, by_place,
        jnp.broadcast_to(begins[0:1, :], (8, kinds)))
    of_row = dot(bf16(dot(bf16(facts), sorter)), of_kind[...])
    device = of_row[0:1, :].astype(jnp.int32)
    spot = (of_row[1:2, :] + rank).astype(jnp.int32)
    hop = jnp.bitwise_xor(device, me)
    to_far = hop >= half
    i = jnp.where(to_far, hop - half, hop)
    ahead = to_far & (spot < first)
    pitch = near + rest
    slots[...] = jnp.where(ahead, -1, i * pitch + jnp.where(to_far, near - first + spot, spot))
    begin = jnp.where(to_far, far_at + i * rest, near_at + i * near)
    index = jnp.where(ahead, i * first, begin) + jnp.where(ahead | ~to_far, spot, spot - first)
    line = jnp.right_shift(index, 7) - jnp.right_shift(begin, 7)
    high[...] = jnp.where(
        to_far, peers + 3 * i + jnp.where(ahead, 0, 1 + line), 2 * i + line)
    low[...] = jnp.bitwise_and(index, LANES - 1)

    def pack_pair(i):
        return pack(slots[...] - i * pitch, pitch)

    both = pack_pair(0)
    recv[near_at:near_at + near] = both[0:near]
    send[far_at:far_at + rest] = both[near:pitch]
    far_copy(0).start()

    @pl.loop(1, half)
    def _(i):
        both = pack_pair(i)
        send[pl.ds(pl.multiple_of(far_at + i * rest, 16), rest)] = both[near:pitch]

        @pl.when(i < AHEAD)
        def _():
            far_copy(i).start()

        send[pl.ds(pl.multiple_of(near_at + i * near, 16), near)] = both[0:near]
        near_copy(i).start()

    value = bf16(lax.broadcasted_iota(jnp.int32, (kinds, LANES), 0) + 1)

    def label(block, begin, count):
        position = lax.broadcasted_iota(jnp.int32, (count, kinds), 0) + begin
        position = position.astype(jnp.float32)
        inside = (position >= low_edge[pl.ds(block, 1), :]) & (position < high_edge[pl.ds(block, 1), :])
        return dot(bf16(inside), value)

    @pl.loop(0, half)
    def _(i):
        id_col[pl.ds(pl.multiple_of(i * first, 16), first)] = label(2 * i + 1, 0, first)
        id_col[pl.ds(pl.multiple_of(near_at + i * near, 16), near)] = label(2 * i, 0, near)
        id_col[pl.ds(pl.multiple_of(far_at + i * rest, 16), rest)] = label(2 * i + 1, first, rest)

    one = bf16(lax.broadcasted_iota(jnp.int32, (8, LANES), 1) == 0)
    for at in range(0, total, LANES):
        id_row[:, at:at + LANES] = dot(one, bf16(id_col[at:at + LANES]), ((1,), (1,)))

    def score(start, width):
        label = id_row[0:1, start:start + width]
        tile = dot(recv[start:start + width], recv[start:start + width], ((1,), (1,)))
        best = []
        for at in range(0, width, LANES):
            left = lax.broadcasted_iota(jnp.int32, (width, LANES), 0)
            right = lax.broadcasted_iota(jnp.int32, (width, LANES), 1) + at
            same = (id_col[start:start + width] == label[:, at:at + LANES]) & (left != right)
            best.append(fold_rows(jnp.where(same, tile[:, at:at + LANES], -1.0)))

        def strip(at, count, best):
            old = pl.ds(pl.multiple_of(at, LANES), count)
            tile = dot(recv[old], recv[start:start + width], ((1,), (1,)))
            ids = id_col[old]
            run = row_best[old]
            result = []
            for at in range(0, width, LANES):
                kept = jnp.where(ids == label[:, at:at + LANES], tile[:, at:at + LANES], -1.0)
                run = jnp.maximum(run, kept)
                result.append(fold_rows(kept))
            row_best[old] = run
            return jnp.maximum(best, jnp.concatenate(result, axis=1))

        best = jnp.concatenate(best, axis=1)
        best = lax.fori_loop(0, start // STRIP, lambda k, best: strip(k * STRIP, STRIP, best), best)
        if start % STRIP:
            best = strip(start // STRIP * STRIP, start % STRIP, best)
        col_best[:, start:start + width] = best

    @pl.loop(0, half)
    def _(i):
        first_copy(i).wait()

    score(0, near_at)
    done = 0
    for i in range(half):
        if i:
            near_copy(i).wait()
        ready = half * near if i == half - 1 else (i + 1) * near // 256 * 256
        if ready > done:
            score(near_at + done, ready - done)
            done = ready
    done = 0
    for i in range(half):
        far_copy(i).wait()
        if i + AHEAD < half:
            far_copy(i + AHEAD).start()
        ready = (i + 1) * rest // LANES * LANES
        if ready > done:
            score(far_at + done, ready - done)
            done = ready

    for at in range(0, total, LANES):
        best = jnp.maximum(col_best[:, at:at + LANES], fold_rows(row_best[at:at + LANES].T))
        ret_out[at // LANES:at // LANES + 1, :] = jnp.max(best, axis=0, keepdims=True)

    @pl.loop(1, peers)
    def _(block):
        answer(block).start()

    ret_in[0] = ret_out[...]

    @pl.loop(1, groups)
    def _(block):
        warn(block).wait()

    over[...] = jnp.max(over_in[...], axis=0)

    @pl.loop(1, peers)
    def _(block):
        answer(block).wait()

    for i in range(half):
        line = (near_at + i * near) // LANES
        table[2 * i:2 * i + 2, :] = ret_in[2 * i, line:line + 2, :]
        to = peers + 3 * i
        line = i * first // LANES
        table[to:to + 1, :] = ret_in[2 * i + 1, line:line + 1, :]
        line = (far_at + i * rest) // LANES
        table[to + 1:to + 3, :] = ret_in[2 * i + 1, line:line + 2, :]
    left_over = table[...].T
    pieces = []
    for _ in range(3):
        pieces.append(left_over.astype(jnp.bfloat16))
        left_over = left_over - pieces[-1].astype(jnp.float32)
    step = min(rows, 512)
    for start in range(0, rows, step):
        index = lax.broadcasted_iota(jnp.int32, (LANES, step), 0)
        hot = bf16(index == high[:, start:start + step])
        value = sum(dot(p, hot) for p in pieces)
        out[:, start:start + step] = jnp.sum(
            jnp.where(index == low[:, start:start + step], value, 0.0), axis=0, keepdims=True)


def spare_kernel(peers, cap, emb, owner, cluster, out, send, recv, ids_out, ids_in, id_col, row_best, col_best,
                 ret_out, ret_in, slots, table, row_send, row_recv, id_send, id_recv, ret_send, ret_recv):
    me = lax.axis_index("wide")
    rows = emb.shape[0]
    half = peers // 2

    def partner(block):
        hop = block // 2 + (block % 2) * half
        result, bit = 0, 1
        while bit < peers:
            result = result + bit * ((me // bit + hop // bit) % 2)
            bit *= 2
        return result

    def copies(block):
        to = {"wide": partner(block)}
        return (
            pltpu.make_async_remote_copy(
                src_ref=send.at[block], dst_ref=recv.at[block],
                send_sem=row_send.at[block], recv_sem=row_recv.at[block],
                device_id=to, device_id_type=pl.DeviceIdType.MESH),
            pltpu.make_async_remote_copy(
                src_ref=ids_out.at[block], dst_ref=ids_in.at[block],
                send_sem=id_send.at[block], recv_sem=id_recv.at[block],
                device_id=to, device_id_type=pl.DeviceIdType.MESH),
        )

    def answer(block):
        return pltpu.make_async_remote_copy(
            src_ref=ret_out.at[block], dst_ref=ret_in.at[block],
            send_sem=ret_send.at[block], recv_sem=ret_recv.at[block],
            device_id={"wide": partner(block)}, device_id_type=pl.DeviceIdType.MESH)

    barrier = pltpu.get_barrier_semaphore()

    @pl.loop(1, peers)
    def _(block):
        pl.semaphore_signal(
            barrier, inc=1, device_id={"wide": partner(block)},
            device_id_type=pl.DeviceIdType.MESH)

    device = owner[...]
    names_of = cluster[...] + 1

    hop = jnp.bitwise_xor(device, me)
    block_of = jnp.where(hop >= half, 2 * hop - peers + 1, 2 * hop)
    upto = (
        lax.broadcasted_iota(jnp.int32, (LANES, LANES), 0)
        <= lax.broadcasted_iota(jnp.int32, (LANES, LANES), 1)
    ).astype(jnp.float32).astype(jnp.bfloat16)
    seen = jnp.zeros((peers, 1), jnp.float32)
    for start in range(0, rows, LANES):
        part = block_of[:, start:start + LANES]
        hot = (lax.broadcasted_iota(jnp.int32, (peers, LANES), 0) == part).astype(jnp.float32)
        count = jnp.dot(hot.astype(jnp.bfloat16), upto, preferred_element_type=jnp.float32)
        rank = jnp.sum(hot * (count + seen), axis=0, keepdims=True) - 1.0
        slots[:, start:start + LANES] = part * cap + rank.astype(jnp.int32)
        seen = seen + count[:, LANES - 1:LANES]

    def pack(block, row_ref, id_ref):
        key = slots[...] - block * cap
        hot = (lax.broadcasted_iota(jnp.int32, (cap, rows), 0) == key).astype(jnp.float32)
        hot = hot.astype(jnp.bfloat16)
        picked = jnp.dot(hot, emb[...], preferred_element_type=jnp.float32)
        scale = lax.rsqrt(jnp.sum(picked * picked, axis=1, keepdims=True) + 1e-06)
        row_ref[block] = (picked * scale).astype(jnp.bfloat16)
        label = jnp.broadcast_to(names_of.astype(jnp.float32), (8, rows))
        id_ref[block] = lax.dot_general(
            label.astype(jnp.bfloat16), hot, (((1,), (1,)), ((), ())),
            preferred_element_type=jnp.float32)

    pl.semaphore_wait(barrier, peers - 1)

    @pl.loop(1, peers)
    def _(block):
        pack(block, send, ids_out)

        @pl.when(block <= WINDOW)
        def _():
            for copy in copies(block):
                copy.start()

    pack(0, recv, ids_in)

    def score(new):
        label = ids_in[new][0:1, :]
        id_col[new] = jnp.broadcast_to(label, (LANES, cap)).T
        row_best[new] = jnp.full((cap, LANES), -1.0, jnp.float32)
        rhs = recv[new]
        tile = lax.dot_general(
            rhs, rhs, (((1,), (1,)), ((), ())), preferred_element_type=jnp.float32)
        first = []
        for at in range(0, cap, LANES):
            left = lax.broadcasted_iota(jnp.int32, (cap, LANES), 0)
            right = lax.broadcasted_iota(jnp.int32, (cap, LANES), 1) + at
            same = (id_col[new] == label[:, at:at + LANES]) & (left != right)
            first.append(fold_rows(jnp.where(same, tile[:, at:at + LANES], -1.0)))

        def pair(old):
            tile = lax.dot_general(
                recv[old], recv[new], (((1,), (1,)), ((), ())),
                preferred_element_type=jnp.float32)
            ids = id_col[old]
            run = row_best[old]
            result = []
            for at in range(0, cap, LANES):
                kept = jnp.where(ids == label[:, at:at + LANES], tile[:, at:at + LANES], -1.0)
                run = jnp.maximum(run, kept)
                result.append(fold_rows(kept))
            row_best[old] = run
            return jnp.concatenate(result, axis=1)

        def pairs(step, best):
            return jnp.maximum(best, jnp.maximum(pair(2 * step), pair(2 * step + 1)))

        col_best[new] = lax.fori_loop(0, new // 2, pairs, jnp.concatenate(first, axis=1))

        @pl.when(new % 2 == 1)
        def _():
            col_best[new] = jnp.maximum(col_best[new], pair(new - 1))

    score(0)

    @pl.loop(1, peers)
    def _(block):
        for copy in copies(block):
            copy.wait()

        @pl.when(block + WINDOW < peers)
        def _():
            for copy in copies(block + WINDOW):
                copy.start()

        score(block)

    def total(block):
        return jnp.maximum(col_best[block], fold_rows(row_best[block].T))

    @pl.loop(1, peers)
    def _(block):
        ret_out[block] = total(block)
        answer(block).start()

    ret_in[0] = total(0)
    table[...] = jnp.zeros((LANES, LANES), jnp.float32)

    @pl.loop(1, peers)
    def _(block):
        answer(block).wait()

    each = cap // LANES
    for block in range(peers):
        best = jnp.max(ret_in[block], axis=0, keepdims=True)
        for piece in range(each):
            table[block * each + piece:block * each + piece + 1, :] = (
                best[:, piece * LANES:(piece + 1) * LANES])
    rest = table[...].T
    pieces = []
    for _ in range(3):
        pieces.append(rest.astype(jnp.bfloat16))
        rest = rest - pieces[-1].astype(jnp.float32)
    step = min(rows, 512)
    for start in range(0, rows, step):
        slot = slots[:, start:start + step]
        high = jnp.right_shift(slot, 7)
        low = jnp.bitwise_and(slot, LANES - 1)
        index = lax.broadcasted_iota(jnp.int32, (LANES, step), 0)
        hot = (index == high).astype(jnp.float32).astype(jnp.bfloat16)
        value = sum(jnp.dot(p, hot, preferred_element_type=jnp.float32) for p in pieces)
        out[:, start:start + step] = jnp.sum(
            jnp.where(index == low, value, 0.0), axis=0, keepdims=True)


def solution(mesh):
    peers, groups = mesh.shape["wide"], mesh.shape["groups"]
    vmem = pl.BlockSpec(memory_space=pltpu.VMEM)

    def spare_call(embeddings, owner, cluster):
        rows, width = embeddings.shape
        cap = 2 * rows // peers
        return pl.pallas_call(
            functools.partial(spare_kernel, peers, cap),
            out_shape=jax.ShapeDtypeStruct((1, rows), jnp.float32),
            in_specs=[vmem] * 3,
            out_specs=vmem,
            scratch_shapes=[
                pltpu.VMEM((peers, cap, width), jnp.bfloat16),
                pltpu.VMEM((peers, cap, width), jnp.bfloat16),
                pltpu.VMEM((peers, 8, cap), jnp.float32),
                pltpu.VMEM((peers, 8, cap), jnp.float32),
                pltpu.VMEM((peers, cap, LANES), jnp.float32),
                pltpu.VMEM((peers, cap, LANES), jnp.float32),
                pltpu.VMEM((peers, 8, cap), jnp.float32),
                pltpu.VMEM((peers, 8, cap), jnp.float32),
                pltpu.VMEM((peers, 8, cap), jnp.float32),
                pltpu.VMEM((1, rows), jnp.int32),
                pltpu.VMEM((LANES, LANES), jnp.float32),
            ] + [pltpu.SemaphoreType.DMA((peers,))] * 6,
            compiler_params=pltpu.CompilerParams(
                collective_id=1, has_side_effects=True, vmem_limit_bytes=56 << 20),
        )(embeddings, owner, cluster)

    def call(embeddings, owner, cluster):
        rows, width = embeddings.shape
        near, far, first = sizes_of(rows, peers)
        half = peers // 2
        total = half * (near + far)
        lines = (total // LANES + 8) // 8 * 8
        kinds = 8 * peers
        return pl.pallas_call(
            functools.partial(kernel, peers, groups, near, far, first),
            out_shape=[
                jax.ShapeDtypeStruct((1, rows), jnp.float32),
                jax.ShapeDtypeStruct((8, LANES), jnp.float32),
            ],
            in_specs=[vmem] * 3,
            out_specs=[vmem] * 2,
            scratch_shapes=[
                pltpu.VMEM((total, width), jnp.bfloat16),
                pltpu.VMEM((total, width), jnp.bfloat16),
                pltpu.VMEM((total, LANES), jnp.float32),
                pltpu.VMEM((8, total), jnp.float32),
                pltpu.VMEM((total, LANES), jnp.float32),
                pltpu.VMEM((8, total), jnp.float32),
                pltpu.VMEM((lines, LANES), jnp.float32),
                pltpu.VMEM((peers, lines, LANES), jnp.float32),
                pltpu.VMEM((kinds, rows), jnp.bfloat16),
                pltpu.VMEM((1, rows), jnp.int32),
                pltpu.VMEM((1, rows), jnp.int32),
                pltpu.VMEM((1, rows), jnp.int32),
                pltpu.VMEM((LANES, LANES), jnp.float32),
                pltpu.VMEM((peers, kinds), jnp.float32),
                pltpu.VMEM((peers, kinds), jnp.float32),
                pltpu.VMEM((8, kinds), jnp.float32),
                pltpu.VMEM((peers, 8, kinds), jnp.float32),
                pltpu.VMEM((peers, kinds), jnp.float32),
                pltpu.VMEM((kinds, peers, LANES), jnp.float32),
                pltpu.VMEM((kinds, LANES), jnp.float32),
                pltpu.VMEM((8, LANES), jnp.float32),
                pltpu.VMEM((groups, 8, LANES), jnp.float32),
            ] + [pltpu.SemaphoreType.DMA((half,))] * 6
            + [pltpu.SemaphoreType.DMA((peers,))] * 4
            + [pltpu.SemaphoreType.DMA((groups,))] * 2,
            compiler_params=pltpu.CompilerParams(
                collective_id=0, has_side_effects=True, vmem_limit_bytes=56 << 20),
        )(embeddings, owner, cluster)

    def per_device(embeddings, row_owner, row_cluster):
        rows = embeddings.shape[0]
        args = (embeddings, row_owner.reshape(1, rows), row_cluster.reshape(1, rows))
        best, over = call(*args)
        best = lax.cond(over[0, 0] > 0, lambda: spare_call(*args), lambda: best)
        return best.reshape(rows)

    return jax.shard_map(
        per_device,
        mesh=mesh,
        in_specs=(P(("groups", "wide"), None), P(("groups", "wide"), None), P(("groups", "wide"))),
        out_specs=P(("groups", "wide")),
        check_vma=False,
    )
```

```python
import functools

import jax
import jax.numpy as jnp
from jax import lax
from jax.experimental import pallas as pl
from jax.experimental.pallas import tpu as pltpu
from jax.sharding import PartitionSpec as P

WINDOW = 6
AHEAD = 4
BATCH = 4
STRIP = 512
LANES = 128
NEAR_FROM = 2
NEAR_STEP = 2
FINE = 1


def fold_rows(tile):
    return jnp.max(tile.reshape(tile.shape[0] // 8, 8, tile.shape[1]), axis=0)


def spread(group, groups, block):
    return lax.rem(group + block, groups)


def sizes_of(rows, peers):
    cap = 2 * rows // peers
    far = (cap * 9 // 16 + 15) // 16 * 16
    near = (cap * 10 // 16 + 15) // 16 * 16
    first = far * 2 // 9 // 16 * 16
    return near, far, first


def bf16(x):
    return x.astype(jnp.float32).astype(jnp.bfloat16)


def dot(a, b, contract=((1,), (0,))):
    return lax.dot_general(a, b, (contract, ((), ())), preferred_element_type=jnp.float32)


def kernel(peers, groups, near, far, first, emb, owner, cluster, out, over,
           send, recv, id_col, id_row, row_best, col_best, bests, ret_out, ret_in, of_kind, slots, high, low, table,
           low_edge, high_edge,
           count_out, count_in, counts, choices, chosen, over_out, over_in,
           first_send, first_recv, near_send, near_recv, far_send, far_recv, ret_send, ret_recv,
           count_send, count_recv, over_send, over_recv):
    me = lax.axis_index("wide")
    group = lax.axis_index("groups")
    rows = emb.shape[0]
    half = peers // 2
    rest = far - first
    near_at = half * first
    far_at = near_at + half * near
    total = far_at + half * rest
    kinds = counts.shape[1]

    def partner(block):
        hop = block // 2 + (block % 2) * half
        result, bit = 0, 1
        while bit < peers:
            result = result + bit * ((me // bit + hop // bit) % 2)
            bit *= 2
        return result

    def remote(src, dst, block, sends, recvs, at):
        return pltpu.make_async_remote_copy(
            src_ref=src, dst_ref=dst, send_sem=sends.at[at], recv_sem=recvs.at[at],
            device_id={"wide": partner(block)}, device_id_type=pl.DeviceIdType.MESH)

    def part(at, count):
        where = pl.ds(pl.multiple_of(at, 16), count)
        return send.at[where], recv.at[where]

    def first_copy(i):
        return remote(*part(i * first, first), 2 * i + 1, first_send, first_recv, i)

    def near_copy(i):
        return remote(*part(near_at + i * near, near), 2 * i, near_send, near_recv, i)

    def far_copy(i):
        return remote(*part(far_at + i * rest, rest), 2 * i + 1, far_send, far_recv, i)

    def answer(block):
        return remote(ret_out.at[block, 0:4], ret_in.at[block, 0:4], block, ret_send, ret_recv, block)

    def tell(block):
        return remote(count_out, count_in.at[block], block, count_send, count_recv, block)

    def warn(block):
        return pltpu.make_async_remote_copy(
            src_ref=over_out, dst_ref=over_in.at[block],
            send_sem=over_send.at[block], recv_sem=over_recv.at[block],
            device_id={"groups": spread(group, groups, block)},
            device_id_type=pl.DeviceIdType.MESH)

    barrier = pltpu.get_barrier_semaphore()

    @pl.loop(1, peers)
    def _(block):
        pl.semaphore_signal(
            barrier, inc=1, device_id={"wide": partner(block)},
            device_id_type=pl.DeviceIdType.MESH)

    @pl.loop(1, groups)
    def _(block):
        pl.semaphore_signal(
            barrier, inc=1, device_id={"groups": spread(group, groups, block)},
            device_id_type=pl.DeviceIdType.MESH)

    kind = owner[...] * (kinds // peers) + cluster[...]
    of_kind[...] = bf16(lax.broadcasted_iota(jnp.int32, (kinds, rows), 0) == kind)
    count_out[...] = dot(jnp.ones((8, rows), jnp.bfloat16), of_kind[...], ((1,), (1,)))
    upto = bf16(
        lax.broadcasted_iota(jnp.int32, (LANES, LANES), 0)
        <= lax.broadcasted_iota(jnp.int32, (LANES, LANES), 1))
    seen = jnp.zeros((kinds, 1), jnp.float32)
    ranks = []
    for start in range(0, rows, LANES):
        hot = of_kind[:, start:start + LANES]
        count = dot(hot, upto)
        ranks.append(jnp.sum(hot.astype(jnp.float32) * (count + seen), axis=0, keepdims=True) - 1.0)
        seen = seen + count[:, LANES - 1:LANES]
    rank = jnp.concatenate(ranks, axis=1)
    table[...] = jnp.zeros((LANES, LANES), jnp.float32)
    ret_out[...] = jnp.zeros(ret_out.shape, jnp.float32)
    bests[...] = jnp.zeros(bests.shape, jnp.float32)
    row_best[...] = jnp.full(row_best.shape, -1.0, jnp.float32)

    pl.semaphore_wait(barrier, peers - 1 + groups - 1)

    @pl.loop(1, peers)
    def _(block):
        tell(block).start()

    count_in[0] = count_out[...]

    @pl.loop(1, peers)
    def _(block):
        tell(block).wait()

    for block in range(peers):
        counts[block:block + 1, :] = count_in[block][0:1, :]

    sizes = jnp.broadcast_to(jnp.sum(counts[...], axis=0, keepdims=True), (kinds, kinds))
    others = sizes.T
    before = (
        lax.broadcasted_iota(jnp.int32, (kinds, kinds), 0)
        < lax.broadcasted_iota(jnp.int32, (kinds, kinds), 1))
    above = (others > sizes) | ((others == sizes) & before)
    place = jnp.sum(above.astype(jnp.float32), axis=0, keepdims=True)
    sorter = bf16(
        lax.broadcasted_iota(jnp.int32, (kinds, kinds), 0) == place.astype(jnp.int32))

    def pack(key, count):
        hot = bf16(lax.broadcasted_iota(jnp.int32, (count, rows), 0) == key)
        picked = dot(hot, emb[...])
        scale = lax.rsqrt(jnp.sum(picked * picked, axis=1, keepdims=True) + 1e-06)
        return (picked * scale).astype(jnp.bfloat16)

    placed = dot(bf16(jnp.broadcast_to(place, (8, kinds))), of_kind[...])[0:1, :].astype(jnp.int32)
    hop = jnp.bitwise_xor(placed, me)
    early = (placed < peers) & (hop >= half) & (rank < first)
    key = jnp.where(early, (hop - half) * first + rank.astype(jnp.int32), -1)
    send[0:near_at] = pack(key, near_at)

    @pl.loop(0, half)
    def _(i):
        first_copy(i).start()

    hit = lax.broadcasted_iota(jnp.int32, (kinds, peers, kinds), 0) == place.astype(jnp.int32)[None]
    lines = bf16(jnp.where(hit, counts[...][None], 0.0))
    choices[...] = dot(
        lines.reshape(kinds * peers, kinds), jnp.ones((kinds, LANES), jnp.bfloat16)
    ).reshape(kinds, peers, LANES)
    lane = lax.broadcasted_iota(jnp.int32, (1, LANES), 1)
    tie = jnp.where(lane < peers, lane, 1 << 22).astype(jnp.float32)

    ranked = dot(bf16(counts[...]), sorter, ((1,), (1,)))
    chosen[0:peers, :] = (
        lax.broadcasted_iota(jnp.int32, (peers, LANES), 0)
        == lax.broadcasted_iota(jnp.int32, (peers, LANES), 1)).astype(jnp.float32)

    source = jnp.bitwise_xor(
        lax.broadcasted_iota(jnp.int32, (peers, kinds), 0) % 2, me // half)
    target = lax.broadcasted_iota(jnp.int32, (peers, kinds), 1)
    is_far = source != target // half
    filled = jnp.where((target < peers) & is_far, jnp.maximum(ranked, first), ranked)
    load = jnp.where(
        target < peers, jnp.where(is_far, filled, filled - (near - far)), 0.0)[:, :LANES]

    def choose(step, load):
        at = peers + step * BATCH
        more = [choices[at + i] for i in range(BATCH)]
        keys = [jnp.max(load + m, axis=0, keepdims=True) * LANES + tie for m in more]
        taken = jnp.zeros((1, LANES), jnp.float32)
        for i in range(BATCH):
            key = keys[i] + taken
            pick = key == jnp.min(key, axis=1, keepdims=True)
            chosen[pl.ds(at + i, 1), :] = pick.astype(jnp.float32)
            load = jnp.where(pick, load + more[i], load)
            taken = jnp.where(pick, 1 << 22, taken)
        return load

    load = lax.fori_loop(0, (kinds - peers) // BATCH, choose, load)
    most = jnp.max(jnp.max(load, axis=1, keepdims=True), axis=0, keepdims=True)
    over_out[...] = jnp.broadcast_to((most > far).astype(jnp.float32), (8, LANES))
    over_in[0] = over_out[...]

    @pl.loop(1, groups)
    def _(block):
        warn(block).start()

    picks = bf16(chosen[...])
    together = dot(picks, picks, ((1,), (1,)))
    begins = dot(bf16(filled), bf16(jnp.where(before, together, 0.0)))
    names = bf16(lax.broadcasted_iota(jnp.int32, (8, LANES), 1))
    by_place = dot(names, picks, ((1,), (1,)))
    mine = by_place[0:1, :].astype(jnp.int32) == me
    low_edge[...] = jnp.where(mine, begins, 0.0)
    high_edge[...] = jnp.where(mine, begins + ranked, 0.0)
    facts = jnp.where(
        lax.broadcasted_iota(jnp.int32, (8, kinds), 0) == 0, by_place,
        jnp.broadcast_to(begins[0:1, :], (8, kinds)))
    of_row = dot(bf16(dot(bf16(facts), sorter)), of_kind[...])
    device = of_row[0:1, :].astype(jnp.int32)
    spot = (of_row[1:2, :] + rank).astype(jnp.int32)
    hop = jnp.bitwise_xor(device, me)
    to_far = hop >= half
    i = jnp.where(to_far, hop - half, hop)
    ahead = to_far & (spot < first)
    pitch = near + rest
    slots[...] = jnp.where(ahead, -1, i * pitch + jnp.where(to_far, near - first + spot, spot))
    begin = jnp.where(to_far, far_at + i * rest, near_at + i * near)
    index = jnp.where(ahead, i * first, begin) + jnp.where(ahead | ~to_far, spot, spot - first)
    line = jnp.right_shift(index, 7) - jnp.right_shift(begin, 7)
    high[...] = jnp.where(
        to_far, peers + 3 * i + jnp.where(ahead, 0, 1 + line), 2 * i + line)
    low[...] = jnp.bitwise_and(index, LANES - 1)

    def pack_pair(i):
        return pack(slots[...] - i * pitch, pitch)

    both = pack_pair(0)
    recv[near_at:near_at + near] = both[0:near]
    send[far_at:far_at + rest] = both[near:pitch]
    far_copy(0).start()

    @pl.loop(1, half)
    def _(i):
        both = pack_pair(i)
        send[pl.ds(pl.multiple_of(far_at + i * rest, 16), rest)] = both[near:pitch]

        @pl.when(i < AHEAD)
        def _():
            far_copy(i).start()

        send[pl.ds(pl.multiple_of(near_at + i * near, 16), near)] = both[0:near]
        near_copy(i).start()

    value = bf16(lax.broadcasted_iota(jnp.int32, (kinds, LANES), 0) + 1)

    def label(block, begin, count):
        position = lax.broadcasted_iota(jnp.int32, (count, kinds), 0) + begin
        position = position.astype(jnp.float32)
        inside = (position >= low_edge[pl.ds(block, 1), :]) & (position < high_edge[pl.ds(block, 1), :])
        return dot(bf16(inside), value)

    @pl.loop(0, half)
    def _(i):
        id_col[pl.ds(pl.multiple_of(i * first, 16), first)] = label(2 * i + 1, 0, first)
        id_col[pl.ds(pl.multiple_of(near_at + i * near, 16), near)] = label(2 * i, 0, near)
        id_col[pl.ds(pl.multiple_of(far_at + i * rest, 16), rest)] = label(2 * i + 1, first, rest)

    one = bf16(lax.broadcasted_iota(jnp.int32, (8, LANES), 1) == 0)
    for at in range(0, total, LANES):
        id_row[:, at:at + LANES] = dot(one, bf16(id_col[at:at + LANES]), ((1,), (1,)))

    def score(start, width, done):
        label = id_row[0:1, start:start + width]
        tile = dot(recv[start:start + width], recv[start:start + width], ((1,), (1,)))
        best = []
        for at in range(0, width, LANES):
            left = lax.broadcasted_iota(jnp.int32, (width, LANES), 0)
            right = lax.broadcasted_iota(jnp.int32, (width, LANES), 1) + at
            same = (id_col[start:start + width] == label[:, at:at + LANES]) & (left != right)
            best.append(fold_rows(jnp.where(same, tile[:, at:at + LANES], -1.0)))

        def strip(at, count, best):
            old = pl.ds(pl.multiple_of(at, LANES), count)
            tile = dot(recv[old], recv[start:start + width], ((1,), (1,)))
            ids = id_col[old]
            run = row_best[old]
            result = []
            for at in range(0, width, LANES):
                kept = jnp.where(ids == label[:, at:at + LANES], tile[:, at:at + LANES], -1.0)
                run = jnp.maximum(run, kept)
                result.append(fold_rows(kept))
            row_best[old] = run
            return jnp.maximum(best, jnp.concatenate(result, axis=1))

        best = jnp.concatenate(best, axis=1)
        for at, end in done:
            count = (end - at) // STRIP
            best = lax.fori_loop(
                0, count, lambda k, best, at=at: strip(at + k * STRIP, STRIP, best), best)
            if (end - at) % STRIP:
                best = strip(at + count * STRIP, (end - at) % STRIP, best)
        col_best[:, start:start + width] = best

    @pl.loop(0, half)
    def _(i):
        first_copy(i).wait()

    score(0, near_at, [])
    near_done, far_done, near_next, far_next = near_at, far_at, 1, 0

    def take_near(count, near_done, near_next):
        for _ in range(count):
            if near_next < half:
                near_copy(near_next).wait()
                near_next += 1
        ready = near_at + near_next * near
        ready = ready if near_next == half else ready // 256 * 256
        while near_done < ready:
            width = min(256, ready - near_done)
            score(near_done, width, [(0, near_done), (far_at, far_done)])
            near_done += width
        return near_done, near_next

    near_done, near_next = take_near(half // 2 - 1, near_done, near_next)
    for i in range(half):
        far_copy(i).wait_send()
        if i + AHEAD < half:
            far_copy(i + AHEAD).start()
        if i >= NEAR_FROM:
            near_done, near_next = take_near(NEAR_STEP, near_done, near_next)
        far_copy(i).wait_recv()
        ready = far_at + (i + 1) * rest
        ready = ready // LANES * LANES if i >= half - FINE else ready // 256 * 256
        while far_done < ready:
            width = min(256, ready - far_done)
            score(far_done, width, [(0, near_done), (far_at, far_done)])
            far_done += width

    for at in range(0, total, LANES):
        best = jnp.maximum(col_best[:, at:at + LANES], fold_rows(row_best[at:at + LANES].T))
        bests[at // LANES:at // LANES + 1, :] = jnp.max(best, axis=0, keepdims=True)
    for i in range(half):
        line = (near_at + i * near) // LANES
        ret_out[2 * i, 0:2] = bests[line:line + 2]
        line = i * first // LANES
        ret_out[2 * i + 1, 0:1] = bests[line:line + 1]
        line = (far_at + i * rest) // LANES
        ret_out[2 * i + 1, 1:3] = bests[line:line + 2]

    @pl.loop(1, peers)
    def _(block):
        answer(block).start()

    ret_in[0] = ret_out[0]

    @pl.loop(1, groups)
    def _(block):
        warn(block).wait()

    over[...] = jnp.max(over_in[...], axis=0)

    @pl.loop(1, peers)
    def _(block):
        answer(block).wait()

    for i in range(half):
        table[2 * i:2 * i + 2, :] = ret_in[2 * i, 0:2]
        table[peers + 3 * i:peers + 3 * i + 3, :] = ret_in[2 * i + 1, 0:3]
    left_over = table[...].T
    pieces = []
    for _ in range(3):
        pieces.append(left_over.astype(jnp.bfloat16))
        left_over = left_over - pieces[-1].astype(jnp.float32)
    step = min(rows, 512)
    for start in range(0, rows, step):
        index = lax.broadcasted_iota(jnp.int32, (LANES, step), 0)
        hot = bf16(index == high[:, start:start + step])
        value = sum(dot(p, hot) for p in pieces)
        out[:, start:start + step] = jnp.sum(
            jnp.where(index == low[:, start:start + step], value, 0.0), axis=0, keepdims=True)


def spare_kernel(peers, cap, emb, owner, cluster, out, send, recv, ids_out, ids_in, id_col, row_best, col_best,
                 ret_out, ret_in, slots, table, row_send, row_recv, id_send, id_recv, ret_send, ret_recv):
    me = lax.axis_index("wide")
    rows = emb.shape[0]
    half = peers // 2

    def partner(block):
        hop = block // 2 + (block % 2) * half
        result, bit = 0, 1
        while bit < peers:
            result = result + bit * ((me // bit + hop // bit) % 2)
            bit *= 2
        return result

    def copies(block):
        to = {"wide": partner(block)}
        return (
            pltpu.make_async_remote_copy(
                src_ref=send.at[block], dst_ref=recv.at[block],
                send_sem=row_send.at[block], recv_sem=row_recv.at[block],
                device_id=to, device_id_type=pl.DeviceIdType.MESH),
            pltpu.make_async_remote_copy(
                src_ref=ids_out.at[block], dst_ref=ids_in.at[block],
                send_sem=id_send.at[block], recv_sem=id_recv.at[block],
                device_id=to, device_id_type=pl.DeviceIdType.MESH),
        )

    def answer(block):
        return pltpu.make_async_remote_copy(
            src_ref=ret_out.at[block], dst_ref=ret_in.at[block],
            send_sem=ret_send.at[block], recv_sem=ret_recv.at[block],
            device_id={"wide": partner(block)}, device_id_type=pl.DeviceIdType.MESH)

    barrier = pltpu.get_barrier_semaphore()

    @pl.loop(1, peers)
    def _(block):
        pl.semaphore_signal(
            barrier, inc=1, device_id={"wide": partner(block)},
            device_id_type=pl.DeviceIdType.MESH)

    device = owner[...]
    names_of = cluster[...] + 1

    hop = jnp.bitwise_xor(device, me)
    block_of = jnp.where(hop >= half, 2 * hop - peers + 1, 2 * hop)
    upto = (
        lax.broadcasted_iota(jnp.int32, (LANES, LANES), 0)
        <= lax.broadcasted_iota(jnp.int32, (LANES, LANES), 1)
    ).astype(jnp.float32).astype(jnp.bfloat16)
    seen = jnp.zeros((peers, 1), jnp.float32)
    for start in range(0, rows, LANES):
        part = block_of[:, start:start + LANES]
        hot = (lax.broadcasted_iota(jnp.int32, (peers, LANES), 0) == part).astype(jnp.float32)
        count = jnp.dot(hot.astype(jnp.bfloat16), upto, preferred_element_type=jnp.float32)
        rank = jnp.sum(hot * (count + seen), axis=0, keepdims=True) - 1.0
        slots[:, start:start + LANES] = part * cap + rank.astype(jnp.int32)
        seen = seen + count[:, LANES - 1:LANES]

    def pack(block, row_ref, id_ref):
        key = slots[...] - block * cap
        hot = (lax.broadcasted_iota(jnp.int32, (cap, rows), 0) == key).astype(jnp.float32)
        hot = hot.astype(jnp.bfloat16)
        picked = jnp.dot(hot, emb[...], preferred_element_type=jnp.float32)
        scale = lax.rsqrt(jnp.sum(picked * picked, axis=1, keepdims=True) + 1e-06)
        row_ref[block] = (picked * scale).astype(jnp.bfloat16)
        label = jnp.broadcast_to(names_of.astype(jnp.float32), (8, rows))
        id_ref[block] = lax.dot_general(
            label.astype(jnp.bfloat16), hot, (((1,), (1,)), ((), ())),
            preferred_element_type=jnp.float32)

    pl.semaphore_wait(barrier, peers - 1)

    @pl.loop(1, peers)
    def _(block):
        pack(block, send, ids_out)

        @pl.when(block <= WINDOW)
        def _():
            for copy in copies(block):
                copy.start()

    pack(0, recv, ids_in)

    def score(new):
        label = ids_in[new][0:1, :]
        id_col[new] = jnp.broadcast_to(label, (LANES, cap)).T
        row_best[new] = jnp.full((cap, LANES), -1.0, jnp.float32)
        rhs = recv[new]
        tile = lax.dot_general(
            rhs, rhs, (((1,), (1,)), ((), ())), preferred_element_type=jnp.float32)
        first = []
        for at in range(0, cap, LANES):
            left = lax.broadcasted_iota(jnp.int32, (cap, LANES), 0)
            right = lax.broadcasted_iota(jnp.int32, (cap, LANES), 1) + at
            same = (id_col[new] == label[:, at:at + LANES]) & (left != right)
            first.append(fold_rows(jnp.where(same, tile[:, at:at + LANES], -1.0)))

        def pair(old):
            tile = lax.dot_general(
                recv[old], recv[new], (((1,), (1,)), ((), ())),
                preferred_element_type=jnp.float32)
            ids = id_col[old]
            run = row_best[old]
            result = []
            for at in range(0, cap, LANES):
                kept = jnp.where(ids == label[:, at:at + LANES], tile[:, at:at + LANES], -1.0)
                run = jnp.maximum(run, kept)
                result.append(fold_rows(kept))
            row_best[old] = run
            return jnp.concatenate(result, axis=1)

        def pairs(step, best):
            return jnp.maximum(best, jnp.maximum(pair(2 * step), pair(2 * step + 1)))

        col_best[new] = lax.fori_loop(0, new // 2, pairs, jnp.concatenate(first, axis=1))

        @pl.when(new % 2 == 1)
        def _():
            col_best[new] = jnp.maximum(col_best[new], pair(new - 1))

    score(0)

    @pl.loop(1, peers)
    def _(block):
        for copy in copies(block):
            copy.wait()

        @pl.when(block + WINDOW < peers)
        def _():
            for copy in copies(block + WINDOW):
                copy.start()

        score(block)

    def total(block):
        return jnp.maximum(col_best[block], fold_rows(row_best[block].T))

    @pl.loop(1, peers)
    def _(block):
        ret_out[block] = total(block)
        answer(block).start()

    ret_in[0] = total(0)
    table[...] = jnp.zeros((LANES, LANES), jnp.float32)

    @pl.loop(1, peers)
    def _(block):
        answer(block).wait()

    each = cap // LANES
    for block in range(peers):
        best = jnp.max(ret_in[block], axis=0, keepdims=True)
        for piece in range(each):
            table[block * each + piece:block * each + piece + 1, :] = (
                best[:, piece * LANES:(piece + 1) * LANES])
    rest = table[...].T
    pieces = []
    for _ in range(3):
        pieces.append(rest.astype(jnp.bfloat16))
        rest = rest - pieces[-1].astype(jnp.float32)
    step = min(rows, 512)
    for start in range(0, rows, step):
        slot = slots[:, start:start + step]
        high = jnp.right_shift(slot, 7)
        low = jnp.bitwise_and(slot, LANES - 1)
        index = lax.broadcasted_iota(jnp.int32, (LANES, step), 0)
        hot = (index == high).astype(jnp.float32).astype(jnp.bfloat16)
        value = sum(jnp.dot(p, hot, preferred_element_type=jnp.float32) for p in pieces)
        out[:, start:start + step] = jnp.sum(
            jnp.where(index == low, value, 0.0), axis=0, keepdims=True)


def solution(mesh):
    peers, groups = mesh.shape["wide"], mesh.shape["groups"]
    vmem = pl.BlockSpec(memory_space=pltpu.VMEM)

    def spare_call(embeddings, owner, cluster):
        rows, width = embeddings.shape
        cap = 2 * rows // peers
        return pl.pallas_call(
            functools.partial(spare_kernel, peers, cap),
            out_shape=jax.ShapeDtypeStruct((1, rows), jnp.float32),
            in_specs=[vmem] * 3,
            out_specs=vmem,
            scratch_shapes=[
                pltpu.VMEM((peers, cap, width), jnp.bfloat16),
                pltpu.VMEM((peers, cap, width), jnp.bfloat16),
                pltpu.VMEM((peers, 8, cap), jnp.float32),
                pltpu.VMEM((peers, 8, cap), jnp.float32),
                pltpu.VMEM((peers, cap, LANES), jnp.float32),
                pltpu.VMEM((peers, cap, LANES), jnp.float32),
                pltpu.VMEM((peers, 8, cap), jnp.float32),
                pltpu.VMEM((peers, 8, cap), jnp.float32),
                pltpu.VMEM((peers, 8, cap), jnp.float32),
                pltpu.VMEM((1, rows), jnp.int32),
                pltpu.VMEM((LANES, LANES), jnp.float32),
            ] + [pltpu.SemaphoreType.DMA((peers,))] * 6,
            compiler_params=pltpu.CompilerParams(
                collective_id=1, has_side_effects=True, vmem_limit_bytes=56 << 20),
        )(embeddings, owner, cluster)

    def call(embeddings, owner, cluster):
        rows, width = embeddings.shape
        near, far, first = sizes_of(rows, peers)
        half = peers // 2
        total = half * (near + far)
        lines = (total // LANES + 8) // 8 * 8
        kinds = 8 * peers
        return pl.pallas_call(
            functools.partial(kernel, peers, groups, near, far, first),
            out_shape=[
                jax.ShapeDtypeStruct((1, rows), jnp.float32),
                jax.ShapeDtypeStruct((8, LANES), jnp.float32),
            ],
            in_specs=[vmem] * 3,
            out_specs=[vmem] * 2,
            scratch_shapes=[
                pltpu.VMEM((total, width), jnp.bfloat16),
                pltpu.VMEM((total, width), jnp.bfloat16),
                pltpu.VMEM((total, LANES), jnp.float32),
                pltpu.VMEM((8, total), jnp.float32),
                pltpu.VMEM((total, LANES), jnp.float32),
                pltpu.VMEM((8, total), jnp.float32),
                pltpu.VMEM((lines, LANES), jnp.float32),
                pltpu.VMEM((peers, 8, LANES), jnp.float32),
                pltpu.VMEM((peers, 8, LANES), jnp.float32),
                pltpu.VMEM((kinds, rows), jnp.bfloat16),
                pltpu.VMEM((1, rows), jnp.int32),
                pltpu.VMEM((1, rows), jnp.int32),
                pltpu.VMEM((1, rows), jnp.int32),
                pltpu.VMEM((LANES, LANES), jnp.float32),
                pltpu.VMEM((peers, kinds), jnp.float32),
                pltpu.VMEM((peers, kinds), jnp.float32),
                pltpu.VMEM((8, kinds), jnp.float32),
                pltpu.VMEM((peers, 8, kinds), jnp.float32),
                pltpu.VMEM((peers, kinds), jnp.float32),
                pltpu.VMEM((kinds, peers, LANES), jnp.float32),
                pltpu.VMEM((kinds, LANES), jnp.float32),
                pltpu.VMEM((8, LANES), jnp.float32),
                pltpu.VMEM((groups, 8, LANES), jnp.float32),
            ] + [pltpu.SemaphoreType.DMA((half,))] * 6
            + [pltpu.SemaphoreType.DMA((peers,))] * 4
            + [pltpu.SemaphoreType.DMA((groups,))] * 2,
            compiler_params=pltpu.CompilerParams(
                collective_id=0, has_side_effects=True, vmem_limit_bytes=56 << 20),
        )(embeddings, owner, cluster)

    def per_device(embeddings, row_owner, row_cluster):
        rows = embeddings.shape[0]
        args = (embeddings, row_owner.reshape(1, rows), row_cluster.reshape(1, rows))
        best, over = call(*args)
        best = lax.cond(over[0, 0] > 0, lambda: spare_call(*args), lambda: best)
        return best.reshape(rows)

    return jax.shard_map(
        per_device,
        mesh=mesh,
        in_specs=(P(("groups", "wide"), None), P(("groups", "wide"), None), P(("groups", "wide"))),
        out_specs=P(("groups", "wide")),
        check_vma=False,
    )
```

```python
import functools

import jax
import jax.numpy as jnp
from jax import lax
from jax.experimental import pallas as pl
from jax.experimental.pallas import tpu as pltpu
from jax.sharding import PartitionSpec as P

WINDOW = 6
AHEAD = 4
BATCH = 4
STRIP = 512
LANES = 128
NEAR_FROM = 2
NEAR_STEP = 2
FINE = 1


def fold_rows(tile):
    return jnp.max(tile.reshape(tile.shape[0] // 8, 8, tile.shape[1]), axis=0)


def spread(group, groups, block):
    return lax.rem(group + block, groups)


def sizes_of(rows, peers):
    cap = 2 * rows // peers
    far = (cap * 9 // 16 + 15) // 16 * 16
    near = (cap * 10 // 16 + 15) // 16 * 16
    first = far * 2 // 9 // 16 * 16
    return near, far, first


def bf16(x):
    return x.astype(jnp.float32).astype(jnp.bfloat16)


def dot(a, b, contract=((1,), (0,))):
    return lax.dot_general(a, b, (contract, ((), ())), preferred_element_type=jnp.float32)


def kernel(peers, groups, near, far, first, emb_in, owner, cluster, out, over,
           emb, emb_sem, send, recv, id_col, id_row, row_best, col_best, bests, ret_out, ret_in, of_kind, slots, high, low, table,
           low_edge, high_edge,
           count_out, count_in, counts, choices, chosen, over_out, over_in,
           first_send, first_recv, near_send, near_recv, far_send, far_recv, ret_send, ret_recv,
           count_send, count_recv, over_send, over_recv):
    me = lax.axis_index("wide")
    group = lax.axis_index("groups")
    rows = emb.shape[0]
    half = peers // 2
    rest = far - first
    near_at = half * first
    far_at = near_at + half * near
    total = far_at + half * rest
    kinds = counts.shape[1]

    def partner(block):
        hop = block // 2 + (block % 2) * half
        result, bit = 0, 1
        while bit < peers:
            result = result + bit * ((me // bit + hop // bit) % 2)
            bit *= 2
        return result

    def remote(src, dst, block, sends, recvs, at):
        return pltpu.make_async_remote_copy(
            src_ref=src, dst_ref=dst, send_sem=sends.at[at], recv_sem=recvs.at[at],
            device_id={"wide": partner(block)}, device_id_type=pl.DeviceIdType.MESH)

    def part(at, count):
        where = pl.ds(pl.multiple_of(at, 16), count)
        return send.at[where], recv.at[where]

    def first_copy(i):
        return remote(*part(i * first, first), 2 * i + 1, first_send, first_recv, i)

    def near_copy(i):
        return remote(*part(near_at + i * near, near), 2 * i, near_send, near_recv, i)

    def far_copy(i):
        return remote(*part(far_at + i * rest, rest), 2 * i + 1, far_send, far_recv, i)

    def answer(block):
        return remote(ret_out.at[block, 0:4], ret_in.at[block, 0:4], block, ret_send, ret_recv, block)

    def tell(block):
        return remote(count_out, count_in.at[block], block, count_send, count_recv, block)

    def warn(block):
        return pltpu.make_async_remote_copy(
            src_ref=over_out, dst_ref=over_in.at[block],
            send_sem=over_send.at[block], recv_sem=over_recv.at[block],
            device_id={"groups": spread(group, groups, block)},
            device_id_type=pl.DeviceIdType.MESH)

    load_rows = pltpu.make_async_copy(emb_in, emb, emb_sem)
    load_rows.start()
    barrier = pltpu.get_barrier_semaphore()

    @pl.loop(1, peers)
    def _(block):
        pl.semaphore_signal(
            barrier, inc=1, device_id={"wide": partner(block)},
            device_id_type=pl.DeviceIdType.MESH)

    @pl.loop(1, groups)
    def _(block):
        pl.semaphore_signal(
            barrier, inc=1, device_id={"groups": spread(group, groups, block)},
            device_id_type=pl.DeviceIdType.MESH)

    kind = owner[...] * (kinds // peers) + cluster[...]
    of_kind[...] = bf16(lax.broadcasted_iota(jnp.int32, (kinds, rows), 0) == kind)
    count_out[...] = dot(jnp.ones((8, rows), jnp.bfloat16), of_kind[...], ((1,), (1,)))

    pl.semaphore_wait(barrier, peers - 1 + groups - 1)
    load_rows.wait()

    @pl.loop(1, peers)
    def _(block):
        tell(block).start()

    count_in[0] = count_out[...]

    upto = bf16(
        lax.broadcasted_iota(jnp.int32, (LANES, LANES), 0)
        <= lax.broadcasted_iota(jnp.int32, (LANES, LANES), 1))
    seen = jnp.zeros((kinds, 1), jnp.float32)
    ranks = []
    for start in range(0, rows, LANES):
        hot = of_kind[:, start:start + LANES]
        count = dot(hot, upto)
        ranks.append(jnp.sum(hot.astype(jnp.float32) * (count + seen), axis=0, keepdims=True) - 1.0)
        seen = seen + count[:, LANES - 1:LANES]
    rank = jnp.concatenate(ranks, axis=1)
    table[...] = jnp.zeros((LANES, LANES), jnp.float32)
    ret_out[...] = jnp.zeros(ret_out.shape, jnp.float32)
    bests[...] = jnp.zeros(bests.shape, jnp.float32)
    row_best[...] = jnp.full(row_best.shape, -1.0, jnp.float32)

    @pl.loop(1, peers)
    def _(block):
        tell(block).wait()

    for block in range(peers):
        counts[block:block + 1, :] = count_in[block][0:1, :]

    sizes = jnp.broadcast_to(jnp.sum(counts[...], axis=0, keepdims=True), (kinds, kinds))
    others = sizes.T
    before = (
        lax.broadcasted_iota(jnp.int32, (kinds, kinds), 0)
        < lax.broadcasted_iota(jnp.int32, (kinds, kinds), 1))
    above = (others > sizes) | ((others == sizes) & before)
    place = jnp.sum(above.astype(jnp.float32), axis=0, keepdims=True)
    sorter = bf16(
        lax.broadcasted_iota(jnp.int32, (kinds, kinds), 0) == place.astype(jnp.int32))

    def pack(key, count):
        hot = bf16(lax.broadcasted_iota(jnp.int32, (count, rows), 0) == key)
        picked = dot(hot, emb[...])
        scale = lax.rsqrt(jnp.sum(picked * picked, axis=1, keepdims=True) + 1e-06)
        return (picked * scale).astype(jnp.bfloat16)

    placed = dot(bf16(jnp.broadcast_to(place, (8, kinds))), of_kind[...])[0:1, :].astype(jnp.int32)
    hop = jnp.bitwise_xor(placed, me)
    early = (placed < peers) & (hop >= half) & (rank < first)
    key = jnp.where(early, (hop - half) * first + rank.astype(jnp.int32), -1)
    send[0:near_at] = pack(key, near_at)

    @pl.loop(0, half)
    def _(i):
        first_copy(i).start()

    hit = lax.broadcasted_iota(jnp.int32, (kinds, peers, kinds), 0) == place.astype(jnp.int32)[None]
    lines = bf16(jnp.where(hit, counts[...][None], 0.0))
    choices[...] = dot(
        lines.reshape(kinds * peers, kinds), jnp.ones((kinds, LANES), jnp.bfloat16)
    ).reshape(kinds, peers, LANES)
    lane = lax.broadcasted_iota(jnp.int32, (1, LANES), 1)
    tie = jnp.where(lane < peers, lane, 1 << 22).astype(jnp.float32)

    ranked = dot(bf16(counts[...]), sorter, ((1,), (1,)))
    chosen[0:peers, :] = (
        lax.broadcasted_iota(jnp.int32, (peers, LANES), 0)
        == lax.broadcasted_iota(jnp.int32, (peers, LANES), 1)).astype(jnp.float32)

    source = jnp.bitwise_xor(
        lax.broadcasted_iota(jnp.int32, (peers, kinds), 0) % 2, me // half)
    target = lax.broadcasted_iota(jnp.int32, (peers, kinds), 1)
    is_far = source != target // half
    filled = jnp.where((target < peers) & is_far, jnp.maximum(ranked, first), ranked)
    load = jnp.where(
        target < peers, jnp.where(is_far, filled, filled - (near - far)), 0.0)[:, :LANES]

    def choose(step, load):
        at = peers + step * BATCH
        more = [choices[at + i] for i in range(BATCH)]
        keys = [jnp.max(load + m, axis=0, keepdims=True) * LANES + tie for m in more]
        taken = jnp.zeros((1, LANES), jnp.float32)
        for i in range(BATCH):
            key = keys[i] + taken
            pick = key == jnp.min(key, axis=1, keepdims=True)
            chosen[pl.ds(at + i, 1), :] = pick.astype(jnp.float32)
            load = jnp.where(pick, load + more[i], load)
            taken = jnp.where(pick, 1 << 22, taken)
        return load

    load = lax.fori_loop(0, (kinds - peers) // BATCH, choose, load)
    most = jnp.max(jnp.max(load, axis=1, keepdims=True), axis=0, keepdims=True)
    over_out[...] = jnp.broadcast_to((most > far).astype(jnp.float32), (8, LANES))
    over_in[0] = over_out[...]

    @pl.loop(1, groups)
    def _(block):
        warn(block).start()

    picks = bf16(chosen[...])
    together = dot(picks, picks, ((1,), (1,)))
    begins = dot(bf16(filled), bf16(jnp.where(before, together, 0.0)))
    names = bf16(lax.broadcasted_iota(jnp.int32, (8, LANES), 1))
    by_place = dot(names, picks, ((1,), (1,)))
    mine = by_place[0:1, :].astype(jnp.int32) == me
    low_edge[...] = jnp.where(mine, begins, 0.0)
    high_edge[...] = jnp.where(mine, begins + ranked, 0.0)
    facts = jnp.where(
        lax.broadcasted_iota(jnp.int32, (8, kinds), 0) == 0, by_place,
        jnp.broadcast_to(begins[0:1, :], (8, kinds)))
    of_row = dot(bf16(dot(bf16(facts), sorter)), of_kind[...])
    device = of_row[0:1, :].astype(jnp.int32)
    spot = (of_row[1:2, :] + rank).astype(jnp.int32)
    hop = jnp.bitwise_xor(device, me)
    to_far = hop >= half
    i = jnp.where(to_far, hop - half, hop)
    ahead = to_far & (spot < first)
    pitch = near + rest
    slots[...] = jnp.where(ahead, -1, i * pitch + jnp.where(to_far, near - first + spot, spot))
    begin = jnp.where(to_far, far_at + i * rest, near_at + i * near)
    index = jnp.where(ahead, i * first, begin) + jnp.where(ahead | ~to_far, spot, spot - first)
    line = jnp.right_shift(index, 7) - jnp.right_shift(begin, 7)
    high[...] = jnp.where(
        to_far, peers + 3 * i + jnp.where(ahead, 0, 1 + line), 2 * i + line)
    low[...] = jnp.bitwise_and(index, LANES - 1)

    def pack_pair(i):
        return pack(slots[...] - i * pitch, pitch)

    both = pack_pair(0)
    recv[near_at:near_at + near] = both[0:near]
    send[far_at:far_at + rest] = both[near:pitch]
    far_copy(0).start()

    @pl.loop(1, half)
    def _(i):
        both = pack_pair(i)
        send[pl.ds(pl.multiple_of(far_at + i * rest, 16), rest)] = both[near:pitch]

        @pl.when(i < AHEAD)
        def _():
            far_copy(i).start()

        send[pl.ds(pl.multiple_of(near_at + i * near, 16), near)] = both[0:near]
        near_copy(i).start()

    value = bf16(lax.broadcasted_iota(jnp.int32, (kinds, LANES), 0) + 1)

    def label(block, begin, count):
        position = lax.broadcasted_iota(jnp.int32, (count, kinds), 0) + begin
        position = position.astype(jnp.float32)
        inside = (position >= low_edge[pl.ds(block, 1), :]) & (position < high_edge[pl.ds(block, 1), :])
        return dot(bf16(inside), value)

    @pl.loop(0, half)
    def _(i):
        id_col[pl.ds(pl.multiple_of(i * first, 16), first)] = label(2 * i + 1, 0, first)
        id_col[pl.ds(pl.multiple_of(near_at + i * near, 16), near)] = label(2 * i, 0, near)
        id_col[pl.ds(pl.multiple_of(far_at + i * rest, 16), rest)] = label(2 * i + 1, first, rest)

    one = bf16(lax.broadcasted_iota(jnp.int32, (8, LANES), 1) == 0)
    for at in range(0, total, LANES):
        id_row[:, at:at + LANES] = dot(one, bf16(id_col[at:at + LANES]), ((1,), (1,)))

    def score(start, width, done):
        label = id_row[0:1, start:start + width]
        tile = dot(recv[start:start + width], recv[start:start + width], ((1,), (1,)))
        best = []
        for at in range(0, width, LANES):
            left = lax.broadcasted_iota(jnp.int32, (width, LANES), 0)
            right = lax.broadcasted_iota(jnp.int32, (width, LANES), 1) + at
            same = (id_col[start:start + width] == label[:, at:at + LANES]) & (left != right)
            best.append(fold_rows(jnp.where(same, tile[:, at:at + LANES], -1.0)))

        def strip(at, count, best):
            old = pl.ds(pl.multiple_of(at, LANES), count)
            tile = dot(recv[old], recv[start:start + width], ((1,), (1,)))
            ids = id_col[old]
            run = row_best[old]
            result = []
            for at in range(0, width, LANES):
                kept = jnp.where(ids == label[:, at:at + LANES], tile[:, at:at + LANES], -1.0)
                run = jnp.maximum(run, kept)
                result.append(fold_rows(kept))
            row_best[old] = run
            return jnp.maximum(best, jnp.concatenate(result, axis=1))

        best = jnp.concatenate(best, axis=1)
        for at, end in done:
            count = (end - at) // STRIP
            best = lax.fori_loop(
                0, count, lambda k, best, at=at: strip(at + k * STRIP, STRIP, best), best)
            if (end - at) % STRIP:
                best = strip(at + count * STRIP, (end - at) % STRIP, best)
        col_best[:, start:start + width] = best

    @pl.loop(0, half)
    def _(i):
        first_copy(i).wait()

    score(0, near_at, [])
    near_done, far_done, near_next, far_next = near_at, far_at, 1, 0

    def take_near(count, near_done, near_next):
        for _ in range(count):
            if near_next < half:
                near_copy(near_next).wait()
                near_next += 1
        ready = near_at + near_next * near
        ready = ready if near_next == half else ready // 256 * 256
        while near_done < ready:
            width = min(256, ready - near_done)
            score(near_done, width, [(0, near_done), (far_at, far_done)])
            near_done += width
        return near_done, near_next

    near_done, near_next = take_near(half // 2 - 1, near_done, near_next)
    for i in range(half):
        far_copy(i).wait_send()
        if i + AHEAD < half:
            far_copy(i + AHEAD).start()
        if i >= NEAR_FROM:
            near_done, near_next = take_near(NEAR_STEP, near_done, near_next)
        far_copy(i).wait_recv()
        ready = far_at + (i + 1) * rest
        ready = ready // LANES * LANES if i >= half - FINE else ready // 256 * 256
        while far_done < ready:
            width = min(256, ready - far_done)
            score(far_done, width, [(0, near_done), (far_at, far_done)])
            far_done += width

    for at in range(0, total, LANES):
        best = jnp.maximum(col_best[:, at:at + LANES], fold_rows(row_best[at:at + LANES].T))
        bests[at // LANES:at // LANES + 1, :] = jnp.max(best, axis=0, keepdims=True)
    for i in range(half):
        line = (near_at + i * near) // LANES
        ret_out[2 * i, 0:2] = bests[line:line + 2]
        line = i * first // LANES
        ret_out[2 * i + 1, 0:1] = bests[line:line + 1]
        line = (far_at + i * rest) // LANES
        ret_out[2 * i + 1, 1:3] = bests[line:line + 2]

    @pl.loop(1, peers)
    def _(block):
        answer(block).start()

    ret_in[0] = ret_out[0]

    @pl.loop(1, groups)
    def _(block):
        warn(block).wait()

    over[0, 0] = jnp.max(jnp.max(over_in[...], axis=0)[0:1, 0:1]).astype(jnp.int32)

    @pl.loop(1, peers)
    def _(block):
        answer(block).wait()

    for i in range(half):
        table[2 * i:2 * i + 2, :] = ret_in[2 * i, 0:2]
        table[peers + 3 * i:peers + 3 * i + 3, :] = ret_in[2 * i + 1, 0:3]
    left_over = table[...].T
    pieces = []
    for _ in range(3):
        pieces.append(left_over.astype(jnp.bfloat16))
        left_over = left_over - pieces[-1].astype(jnp.float32)
    step = min(rows, 512)
    for start in range(0, rows, step):
        index = lax.broadcasted_iota(jnp.int32, (LANES, step), 0)
        hot = bf16(index == high[:, start:start + step])
        value = sum(dot(p, hot) for p in pieces)
        out[:, start:start + step] = jnp.sum(
            jnp.where(index == low[:, start:start + step], value, 0.0), axis=0, keepdims=True)


def spare_kernel(peers, cap, emb, owner, cluster, out, send, recv, ids_out, ids_in, id_col, row_best, col_best,
                 ret_out, ret_in, slots, table, row_send, row_recv, id_send, id_recv, ret_send, ret_recv):
    me = lax.axis_index("wide")
    rows = emb.shape[0]
    half = peers // 2

    def partner(block):
        hop = block // 2 + (block % 2) * half
        result, bit = 0, 1
        while bit < peers:
            result = result + bit * ((me // bit + hop // bit) % 2)
            bit *= 2
        return result

    def copies(block):
        to = {"wide": partner(block)}
        return (
            pltpu.make_async_remote_copy(
                src_ref=send.at[block], dst_ref=recv.at[block],
                send_sem=row_send.at[block], recv_sem=row_recv.at[block],
                device_id=to, device_id_type=pl.DeviceIdType.MESH),
            pltpu.make_async_remote_copy(
                src_ref=ids_out.at[block], dst_ref=ids_in.at[block],
                send_sem=id_send.at[block], recv_sem=id_recv.at[block],
                device_id=to, device_id_type=pl.DeviceIdType.MESH),
        )

    def answer(block):
        return pltpu.make_async_remote_copy(
            src_ref=ret_out.at[block], dst_ref=ret_in.at[block],
            send_sem=ret_send.at[block], recv_sem=ret_recv.at[block],
            device_id={"wide": partner(block)}, device_id_type=pl.DeviceIdType.MESH)

    barrier = pltpu.get_barrier_semaphore()

    @pl.loop(1, peers)
    def _(block):
        pl.semaphore_signal(
            barrier, inc=1, device_id={"wide": partner(block)},
            device_id_type=pl.DeviceIdType.MESH)

    device = owner[...]
    names_of = cluster[...] + 1

    hop = jnp.bitwise_xor(device, me)
    block_of = jnp.where(hop >= half, 2 * hop - peers + 1, 2 * hop)
    upto = (
        lax.broadcasted_iota(jnp.int32, (LANES, LANES), 0)
        <= lax.broadcasted_iota(jnp.int32, (LANES, LANES), 1)
    ).astype(jnp.float32).astype(jnp.bfloat16)
    seen = jnp.zeros((peers, 1), jnp.float32)
    for start in range(0, rows, LANES):
        part = block_of[:, start:start + LANES]
        hot = (lax.broadcasted_iota(jnp.int32, (peers, LANES), 0) == part).astype(jnp.float32)
        count = jnp.dot(hot.astype(jnp.bfloat16), upto, preferred_element_type=jnp.float32)
        rank = jnp.sum(hot * (count + seen), axis=0, keepdims=True) - 1.0
        slots[:, start:start + LANES] = part * cap + rank.astype(jnp.int32)
        seen = seen + count[:, LANES - 1:LANES]

    def pack(block, row_ref, id_ref):
        key = slots[...] - block * cap
        hot = (lax.broadcasted_iota(jnp.int32, (cap, rows), 0) == key).astype(jnp.float32)
        hot = hot.astype(jnp.bfloat16)
        picked = jnp.dot(hot, emb[...], preferred_element_type=jnp.float32)
        scale = lax.rsqrt(jnp.sum(picked * picked, axis=1, keepdims=True) + 1e-06)
        row_ref[block] = (picked * scale).astype(jnp.bfloat16)
        label = jnp.broadcast_to(names_of.astype(jnp.float32), (8, rows))
        id_ref[block] = lax.dot_general(
            label.astype(jnp.bfloat16), hot, (((1,), (1,)), ((), ())),
            preferred_element_type=jnp.float32)

    pl.semaphore_wait(barrier, peers - 1)

    @pl.loop(1, peers)
    def _(block):
        pack(block, send, ids_out)

        @pl.when(block <= WINDOW)
        def _():
            for copy in copies(block):
                copy.start()

    pack(0, recv, ids_in)

    def score(new):
        label = ids_in[new][0:1, :]
        id_col[new] = jnp.broadcast_to(label, (LANES, cap)).T
        row_best[new] = jnp.full((cap, LANES), -1.0, jnp.float32)
        rhs = recv[new]
        tile = lax.dot_general(
            rhs, rhs, (((1,), (1,)), ((), ())), preferred_element_type=jnp.float32)
        first = []
        for at in range(0, cap, LANES):
            left = lax.broadcasted_iota(jnp.int32, (cap, LANES), 0)
            right = lax.broadcasted_iota(jnp.int32, (cap, LANES), 1) + at
            same = (id_col[new] == label[:, at:at + LANES]) & (left != right)
            first.append(fold_rows(jnp.where(same, tile[:, at:at + LANES], -1.0)))

        def pair(old):
            tile = lax.dot_general(
                recv[old], recv[new], (((1,), (1,)), ((), ())),
                preferred_element_type=jnp.float32)
            ids = id_col[old]
            run = row_best[old]
            result = []
            for at in range(0, cap, LANES):
                kept = jnp.where(ids == label[:, at:at + LANES], tile[:, at:at + LANES], -1.0)
                run = jnp.maximum(run, kept)
                result.append(fold_rows(kept))
            row_best[old] = run
            return jnp.concatenate(result, axis=1)

        def pairs(step, best):
            return jnp.maximum(best, jnp.maximum(pair(2 * step), pair(2 * step + 1)))

        col_best[new] = lax.fori_loop(0, new // 2, pairs, jnp.concatenate(first, axis=1))

        @pl.when(new % 2 == 1)
        def _():
            col_best[new] = jnp.maximum(col_best[new], pair(new - 1))

    score(0)

    @pl.loop(1, peers)
    def _(block):
        for copy in copies(block):
            copy.wait()

        @pl.when(block + WINDOW < peers)
        def _():
            for copy in copies(block + WINDOW):
                copy.start()

        score(block)

    def total(block):
        return jnp.maximum(col_best[block], fold_rows(row_best[block].T))

    @pl.loop(1, peers)
    def _(block):
        ret_out[block] = total(block)
        answer(block).start()

    ret_in[0] = total(0)
    table[...] = jnp.zeros((LANES, LANES), jnp.float32)

    @pl.loop(1, peers)
    def _(block):
        answer(block).wait()

    each = cap // LANES
    for block in range(peers):
        best = jnp.max(ret_in[block], axis=0, keepdims=True)
        for piece in range(each):
            table[block * each + piece:block * each + piece + 1, :] = (
                best[:, piece * LANES:(piece + 1) * LANES])
    rest = table[...].T
    pieces = []
    for _ in range(3):
        pieces.append(rest.astype(jnp.bfloat16))
        rest = rest - pieces[-1].astype(jnp.float32)
    step = min(rows, 512)
    for start in range(0, rows, step):
        slot = slots[:, start:start + step]
        high = jnp.right_shift(slot, 7)
        low = jnp.bitwise_and(slot, LANES - 1)
        index = lax.broadcasted_iota(jnp.int32, (LANES, step), 0)
        hot = (index == high).astype(jnp.float32).astype(jnp.bfloat16)
        value = sum(jnp.dot(p, hot, preferred_element_type=jnp.float32) for p in pieces)
        out[:, start:start + step] = jnp.sum(
            jnp.where(index == low, value, 0.0), axis=0, keepdims=True)


def solution(mesh):
    peers, groups = mesh.shape["wide"], mesh.shape["groups"]
    vmem = pl.BlockSpec(memory_space=pltpu.VMEM)

    def spare_call(embeddings, owner, cluster):
        rows, width = embeddings.shape
        cap = 2 * rows // peers
        return pl.pallas_call(
            functools.partial(spare_kernel, peers, cap),
            out_shape=jax.ShapeDtypeStruct((1, rows), jnp.float32),
            in_specs=[vmem] * 3,
            out_specs=vmem,
            scratch_shapes=[
                pltpu.VMEM((peers, cap, width), jnp.bfloat16),
                pltpu.VMEM((peers, cap, width), jnp.bfloat16),
                pltpu.VMEM((peers, 8, cap), jnp.float32),
                pltpu.VMEM((peers, 8, cap), jnp.float32),
                pltpu.VMEM((peers, cap, LANES), jnp.float32),
                pltpu.VMEM((peers, cap, LANES), jnp.float32),
                pltpu.VMEM((peers, 8, cap), jnp.float32),
                pltpu.VMEM((peers, 8, cap), jnp.float32),
                pltpu.VMEM((peers, 8, cap), jnp.float32),
                pltpu.VMEM((1, rows), jnp.int32),
                pltpu.VMEM((LANES, LANES), jnp.float32),
            ] + [pltpu.SemaphoreType.DMA((peers,))] * 6,
            compiler_params=pltpu.CompilerParams(
                collective_id=1, has_side_effects=True, vmem_limit_bytes=56 << 20),
        )(embeddings, owner, cluster)

    def call(embeddings, owner, cluster):
        rows, width = embeddings.shape
        near, far, first = sizes_of(rows, peers)
        half = peers // 2
        total = half * (near + far)
        lines = (total // LANES + 8) // 8 * 8
        kinds = 8 * peers
        return pl.pallas_call(
            functools.partial(kernel, peers, groups, near, far, first),
            out_shape=[
                jax.ShapeDtypeStruct((1, rows), jnp.float32),
                jax.ShapeDtypeStruct((1, 1), jnp.int32),
            ],
            in_specs=[pl.BlockSpec(memory_space=pltpu.HBM), vmem, vmem],
            out_specs=[vmem, pl.BlockSpec(memory_space=pltpu.SMEM)],
            scratch_shapes=[
                pltpu.VMEM((rows, width), jnp.bfloat16),
                pltpu.SemaphoreType.DMA(()),
                pltpu.VMEM((total, width), jnp.bfloat16),
                pltpu.VMEM((total, width), jnp.bfloat16),
                pltpu.VMEM((total, LANES), jnp.float32),
                pltpu.VMEM((8, total), jnp.float32),
                pltpu.VMEM((total, LANES), jnp.float32),
                pltpu.VMEM((8, total), jnp.float32),
                pltpu.VMEM((lines, LANES), jnp.float32),
                pltpu.VMEM((peers, 8, LANES), jnp.float32),
                pltpu.VMEM((peers, 8, LANES), jnp.float32),
                pltpu.VMEM((kinds, rows), jnp.bfloat16),
                pltpu.VMEM((1, rows), jnp.int32),
                pltpu.VMEM((1, rows), jnp.int32),
                pltpu.VMEM((1, rows), jnp.int32),
                pltpu.VMEM((LANES, LANES), jnp.float32),
                pltpu.VMEM((peers, kinds), jnp.float32),
                pltpu.VMEM((peers, kinds), jnp.float32),
                pltpu.VMEM((8, kinds), jnp.float32),
                pltpu.VMEM((peers, 8, kinds), jnp.float32),
                pltpu.VMEM((peers, kinds), jnp.float32),
                pltpu.VMEM((kinds, peers, LANES), jnp.float32),
                pltpu.VMEM((kinds, LANES), jnp.float32),
                pltpu.VMEM((8, LANES), jnp.float32),
                pltpu.VMEM((groups, 8, LANES), jnp.float32),
            ] + [pltpu.SemaphoreType.DMA((half,))] * 6
            + [pltpu.SemaphoreType.DMA((peers,))] * 4
            + [pltpu.SemaphoreType.DMA((groups,))] * 2,
            compiler_params=pltpu.CompilerParams(
                collective_id=0, has_side_effects=True, vmem_limit_bytes=56 << 20),
        )(embeddings, owner, cluster)

    def per_device(embeddings, row_owner, row_cluster):
        rows = embeddings.shape[0]
        args = (embeddings, row_owner.reshape(1, rows), row_cluster.reshape(1, rows))
        best, over = call(*args)
        best = lax.cond(over[0, 0] > 0, lambda: spare_call(*args), lambda: best)
        return best.reshape(rows)

    return jax.shard_map(
        per_device,
        mesh=mesh,
        in_specs=(P(("groups", "wide"), None), P(("groups", "wide"), None), P(("groups", "wide"))),
        out_specs=P(("groups", "wide")),
        check_vma=False,
    )
```

```python
import functools

import jax
import jax.numpy as jnp
from jax import lax
from jax.experimental import pallas as pl
from jax.experimental.pallas import tpu as pltpu
from jax.sharding import PartitionSpec as P

WINDOW = 6
AHEAD = 4
BATCH = 4
STRIP = 512
LANES = 128
NEAR_FROM = 2
NEAR_STEP = 2
FINE = 1


def fold_rows(tile):
    return jnp.max(tile.reshape(tile.shape[0] // 8, 8, tile.shape[1]), axis=0)


def spread(group, groups, block):
    return lax.rem(group + block, groups)


def sizes_of(rows, peers):
    cap = 2 * rows // peers
    far = (cap * 9 // 16 + 15) // 16 * 16
    near = (cap * 10 // 16 + 15) // 16 * 16
    first = far * 2 // 9 // 16 * 16
    return near, far, first


def bf16(x):
    return x.astype(jnp.float32).astype(jnp.bfloat16)


def dot(a, b, contract=((1,), (0,))):
    return lax.dot_general(a, b, (contract, ((), ())), preferred_element_type=jnp.float32)


def kernel(peers, groups, near, far, first, emb_in, owner, cluster, out, over,
           emb, emb_sem, of_line, send, recv, id_col, id_row, row_best, col_best, bests, ret_out, ret_in, of_kind, slots, high, low, table,
           low_edge, high_edge,
           count_out, count_in, counts, choices, chosen, over_out, over_in,
           first_send, first_recv, near_send, near_recv, far_send, far_recv, ret_send, ret_recv,
           count_send, count_recv, over_send, over_recv):
    me = lax.axis_index("wide")
    group = lax.axis_index("groups")
    rows = emb.shape[0]
    half = peers // 2
    rest = far - first
    near_at = half * first
    far_at = near_at + half * near
    total = far_at + half * rest
    kinds = counts.shape[1]

    def partner(block):
        hop = block // 2 + (block % 2) * half
        result, bit = 0, 1
        while bit < peers:
            result = result + bit * ((me // bit + hop // bit) % 2)
            bit *= 2
        return result

    def remote(src, dst, block, sends, recvs, at):
        return pltpu.make_async_remote_copy(
            src_ref=src, dst_ref=dst, send_sem=sends.at[at], recv_sem=recvs.at[at],
            device_id={"wide": partner(block)}, device_id_type=pl.DeviceIdType.MESH)

    def part(at, count):
        where = pl.ds(pl.multiple_of(at, 16), count)
        return send.at[where], recv.at[where]

    def first_copy(i):
        return remote(*part(i * first, first), 2 * i + 1, first_send, first_recv, i)

    def near_copy(i):
        return remote(*part(near_at + i * near, near), 2 * i, near_send, near_recv, i)

    def far_copy(i):
        return remote(*part(far_at + i * rest, rest), 2 * i + 1, far_send, far_recv, i)

    def answer(block):
        return remote(ret_out.at[block, 0:4], ret_in.at[block, 0:4], block, ret_send, ret_recv, block)

    def tell(block):
        return remote(count_out, count_in.at[block], block, count_send, count_recv, block)

    def warn(block):
        return pltpu.make_async_remote_copy(
            src_ref=over_out, dst_ref=over_in.at[block],
            send_sem=over_send.at[block], recv_sem=over_recv.at[block],
            device_id={"groups": spread(group, groups, block)},
            device_id_type=pl.DeviceIdType.MESH)

    load_rows = pltpu.make_async_copy(emb_in, emb, emb_sem)
    load_rows.start()
    barrier = pltpu.get_barrier_semaphore()

    @pl.loop(1, peers)
    def _(block):
        pl.semaphore_signal(
            barrier, inc=1, device_id={"wide": partner(block)},
            device_id_type=pl.DeviceIdType.MESH)

    @pl.loop(1, groups)
    def _(block):
        pl.semaphore_signal(
            barrier, inc=1, device_id={"groups": spread(group, groups, block)},
            device_id_type=pl.DeviceIdType.MESH)

    kind = owner[...] * (kinds // peers) + cluster[...]
    of_kind[...] = bf16(lax.broadcasted_iota(jnp.int32, (kinds, rows), 0) == kind)
    count_out[...] = dot(jnp.ones((8, rows), jnp.bfloat16), of_kind[...], ((1,), (1,)))

    pl.semaphore_wait(barrier, peers - 1 + groups - 1)
    load_rows.wait()

    @pl.loop(1, peers)
    def _(block):
        tell(block).start()

    count_in[0] = count_out[...]

    upto = bf16(
        lax.broadcasted_iota(jnp.int32, (LANES, LANES), 0)
        <= lax.broadcasted_iota(jnp.int32, (LANES, LANES), 1))
    seen = jnp.zeros((kinds, 1), jnp.float32)
    ranks = []
    for start in range(0, rows, LANES):
        hot = of_kind[:, start:start + LANES]
        count = dot(hot, upto)
        ranks.append(jnp.sum(hot.astype(jnp.float32) * (count + seen), axis=0, keepdims=True) - 1.0)
        seen = seen + count[:, LANES - 1:LANES]
    rank = jnp.concatenate(ranks, axis=1)
    table[...] = jnp.zeros((LANES, LANES), jnp.float32)
    ret_out[...] = jnp.zeros(ret_out.shape, jnp.float32)
    bests[...] = jnp.zeros(bests.shape, jnp.float32)
    row_best[...] = jnp.full(row_best.shape, -1.0, jnp.float32)

    @pl.loop(1, peers)
    def _(block):
        tell(block).wait()

    for block in range(peers):
        counts[block:block + 1, :] = count_in[block][0:1, :]

    sizes = jnp.broadcast_to(jnp.sum(counts[...], axis=0, keepdims=True), (kinds, kinds))
    others = sizes.T
    before = (
        lax.broadcasted_iota(jnp.int32, (kinds, kinds), 0)
        < lax.broadcasted_iota(jnp.int32, (kinds, kinds), 1))
    above = (others > sizes) | ((others == sizes) & before)
    place = jnp.sum(above.astype(jnp.float32), axis=0, keepdims=True)
    sorter = bf16(
        lax.broadcasted_iota(jnp.int32, (kinds, kinds), 0) == place.astype(jnp.int32))

    def pack(key, count):
        hot = bf16(lax.broadcasted_iota(jnp.int32, (count, rows), 0) == key)
        picked = dot(hot, emb[...])
        scale = lax.rsqrt(jnp.sum(picked * picked, axis=1, keepdims=True) + 1e-06)
        return (picked * scale).astype(jnp.bfloat16)

    placed = dot(bf16(jnp.broadcast_to(place, (8, kinds))), of_kind[...])[0:1, :].astype(jnp.int32)
    hop = jnp.bitwise_xor(placed, me)
    early = (placed < peers) & (hop >= half) & (rank < first)
    key = jnp.where(early, (hop - half) * first + rank.astype(jnp.int32), -1)
    send[0:near_at] = pack(key, near_at)

    @pl.loop(0, half)
    def _(i):
        first_copy(i).start()

    hit = lax.broadcasted_iota(jnp.int32, (kinds, peers, kinds), 0) == place.astype(jnp.int32)[None]
    lines = bf16(jnp.where(hit, counts[...][None], 0.0))
    choices[...] = dot(
        lines.reshape(kinds * peers, kinds), jnp.ones((kinds, LANES), jnp.bfloat16)
    ).reshape(kinds, peers, LANES)
    lane = lax.broadcasted_iota(jnp.int32, (1, LANES), 1)
    tie = jnp.where(lane < peers, lane, 1 << 22).astype(jnp.float32)

    ranked = dot(bf16(counts[...]), sorter, ((1,), (1,)))
    chosen[0:peers, :] = (
        lax.broadcasted_iota(jnp.int32, (peers, LANES), 0)
        == lax.broadcasted_iota(jnp.int32, (peers, LANES), 1)).astype(jnp.float32)

    source = jnp.bitwise_xor(
        lax.broadcasted_iota(jnp.int32, (peers, kinds), 0) % 2, me // half)
    target = lax.broadcasted_iota(jnp.int32, (peers, kinds), 1)
    is_far = source != target // half
    filled = jnp.where((target < peers) & is_far, jnp.maximum(ranked, first), ranked)
    load = jnp.where(
        target < peers, jnp.where(is_far, filled, filled - (near - far)), 0.0)[:, :LANES]

    def choose(step, load):
        at = peers + step * BATCH
        more = [choices[at + i] for i in range(BATCH)]
        keys = [jnp.max(load + m, axis=0, keepdims=True) * LANES + tie for m in more]
        taken = jnp.zeros((1, LANES), jnp.float32)
        for i in range(BATCH):
            key = keys[i] + taken
            pick = key == jnp.min(key, axis=1, keepdims=True)
            chosen[pl.ds(at + i, 1), :] = pick.astype(jnp.float32)
            load = jnp.where(pick, load + more[i], load)
            taken = jnp.where(pick, 1 << 22, taken)
        return load

    load = lax.fori_loop(0, (kinds - peers) // BATCH, choose, load)
    most = jnp.max(jnp.max(load, axis=1, keepdims=True), axis=0, keepdims=True)
    over_out[...] = jnp.broadcast_to((most > far).astype(jnp.float32), (8, LANES))
    over_in[0] = over_out[...]

    @pl.loop(1, groups)
    def _(block):
        warn(block).start()

    picks = bf16(chosen[...])
    together = dot(picks, picks, ((1,), (1,)))
    begins = dot(bf16(filled), bf16(jnp.where(before, together, 0.0)))
    names = bf16(lax.broadcasted_iota(jnp.int32, (8, LANES), 1))
    by_place = dot(names, picks, ((1,), (1,)))
    mine = by_place[0:1, :].astype(jnp.int32) == me
    low_edge[...] = jnp.where(mine, begins, 0.0)
    high_edge[...] = jnp.where(mine, begins + ranked, 0.0)
    facts = jnp.where(
        lax.broadcasted_iota(jnp.int32, (8, kinds), 0) == 0, by_place,
        jnp.broadcast_to(begins[0:1, :], (8, kinds)))
    of_row = dot(bf16(dot(bf16(facts), sorter)), of_kind[...])
    device = of_row[0:1, :].astype(jnp.int32)
    spot = (of_row[1:2, :] + rank).astype(jnp.int32)
    hop = jnp.bitwise_xor(device, me)
    to_far = hop >= half
    i = jnp.where(to_far, hop - half, hop)
    ahead = to_far & (spot < first)
    pitch = near + rest
    slots[...] = jnp.where(ahead, -1, i * pitch + jnp.where(to_far, near - first + spot, spot))
    begin = jnp.where(to_far, far_at + i * rest, near_at + i * near)
    index = jnp.where(ahead, i * first, begin) + jnp.where(ahead | ~to_far, spot, spot - first)
    line = jnp.right_shift(index, 7) - jnp.right_shift(begin, 7)
    high[...] = jnp.where(
        to_far, peers + 3 * i + jnp.where(ahead, 0, 1 + line), 2 * i + line)
    low[...] = jnp.bitwise_and(index, LANES - 1)

    def pack_pair(i):
        return pack(slots[...] - i * pitch, pitch)

    both = pack_pair(0)
    recv[near_at:near_at + near] = both[0:near]
    send[far_at:far_at + rest] = both[near:pitch]
    far_copy(0).start()

    @pl.loop(1, half)
    def _(i):
        both = pack_pair(i)
        send[pl.ds(pl.multiple_of(far_at + i * rest, 16), rest)] = both[near:pitch]

        @pl.when(i < AHEAD)
        def _():
            far_copy(i).start()

        send[pl.ds(pl.multiple_of(near_at + i * near, 16), near)] = both[0:near]
        near_copy(i).start()

    value = bf16(lax.broadcasted_iota(jnp.int32, (kinds, LANES), 0) + 1)

    def label(block, begin, count):
        position = lax.broadcasted_iota(jnp.int32, (count, kinds), 0) + begin
        position = position.astype(jnp.float32)
        inside = (position >= low_edge[pl.ds(block, 1), :]) & (position < high_edge[pl.ds(block, 1), :])
        return dot(bf16(inside), value)

    @pl.loop(0, half)
    def _(i):
        id_col[pl.ds(pl.multiple_of(i * first, 16), first)] = label(2 * i + 1, 0, first)
        id_col[pl.ds(pl.multiple_of(near_at + i * near, 16), near)] = label(2 * i, 0, near)
        id_col[pl.ds(pl.multiple_of(far_at + i * rest, 16), rest)] = label(2 * i + 1, first, rest)

    of_line[...] = bf16(lax.broadcasted_iota(jnp.int32, (LANES, rows), 0) == high[...])
    one = bf16(lax.broadcasted_iota(jnp.int32, (8, LANES), 1) == 0)
    for at in range(0, total, LANES):
        id_row[:, at:at + LANES] = dot(one, bf16(id_col[at:at + LANES]), ((1,), (1,)))

    def score(start, width, done):
        label = id_row[0:1, start:start + width]
        tile = dot(recv[start:start + width], recv[start:start + width], ((1,), (1,)))
        best = []
        for at in range(0, width, LANES):
            left = lax.broadcasted_iota(jnp.int32, (width, LANES), 0)
            right = lax.broadcasted_iota(jnp.int32, (width, LANES), 1) + at
            same = (id_col[start:start + width] == label[:, at:at + LANES]) & (left != right)
            best.append(fold_rows(jnp.where(same, tile[:, at:at + LANES], -1.0)))

        def strip(at, count, best):
            old = pl.ds(pl.multiple_of(at, LANES), count)
            tile = dot(recv[old], recv[start:start + width], ((1,), (1,)))
            ids = id_col[old]
            run = row_best[old]
            result = []
            for at in range(0, width, LANES):
                kept = jnp.where(ids == label[:, at:at + LANES], tile[:, at:at + LANES], -1.0)
                run = jnp.maximum(run, kept)
                result.append(fold_rows(kept))
            row_best[old] = run
            return jnp.maximum(best, jnp.concatenate(result, axis=1))

        best = jnp.concatenate(best, axis=1)
        for at, end in done:
            count = (end - at) // STRIP
            best = lax.fori_loop(
                0, count, lambda k, best, at=at: strip(at + k * STRIP, STRIP, best), best)
            if (end - at) % STRIP:
                best = strip(at + count * STRIP, (end - at) % STRIP, best)
        col_best[:, start:start + width] = best

    @pl.loop(0, half)
    def _(i):
        first_copy(i).wait()

    score(0, near_at, [])
    near_done, far_done, near_next, far_next = near_at, far_at, 1, 0

    def take_near(count, near_done, near_next):
        for _ in range(count):
            if near_next < half:
                near_copy(near_next).wait()
                near_next += 1
        ready = near_at + near_next * near
        ready = ready if near_next == half else ready // 256 * 256
        while near_done < ready:
            width = min(256, ready - near_done)
            score(near_done, width, [(0, near_done), (far_at, far_done)])
            near_done += width
        return near_done, near_next

    near_done, near_next = take_near(half // 2 - 1, near_done, near_next)
    for i in range(half):
        far_copy(i).wait_send()
        if i + AHEAD < half:
            far_copy(i + AHEAD).start()
        if i >= NEAR_FROM:
            near_done, near_next = take_near(NEAR_STEP, near_done, near_next)
        far_copy(i).wait_recv()
        ready = far_at + (i + 1) * rest
        ready = ready // LANES * LANES if i >= half - FINE else ready // 256 * 256
        while far_done < ready:
            width = min(256, ready - far_done)
            score(far_done, width, [(0, near_done), (far_at, far_done)])
            far_done += width

    for at in range(0, total, LANES):
        best = jnp.maximum(col_best[:, at:at + LANES], fold_rows(row_best[at:at + LANES].T))
        bests[at // LANES:at // LANES + 1, :] = jnp.max(best, axis=0, keepdims=True)
    for i in range(half):
        line = (near_at + i * near) // LANES
        ret_out[2 * i, 0:2] = bests[line:line + 2]
        line = i * first // LANES
        ret_out[2 * i + 1, 0:1] = bests[line:line + 1]
        line = (far_at + i * rest) // LANES
        ret_out[2 * i + 1, 1:3] = bests[line:line + 2]

    @pl.loop(1, peers)
    def _(block):
        answer(block).start()

    ret_in[0] = ret_out[0]

    @pl.loop(1, groups)
    def _(block):
        warn(block).wait()

    over[0, 0] = jnp.max(jnp.max(over_in[...], axis=0)[0:1, 0:1]).astype(jnp.int32)

    @pl.loop(1, peers)
    def _(block):
        answer(block).wait()

    for i in range(half):
        table[2 * i:2 * i + 2, :] = ret_in[2 * i, 0:2]
        table[peers + 3 * i:peers + 3 * i + 3, :] = ret_in[2 * i + 1, 0:3]
    left_over = table[...].T
    pieces = []
    for _ in range(3):
        pieces.append(left_over.astype(jnp.bfloat16))
        left_over = left_over - pieces[-1].astype(jnp.float32)
    step = min(rows, 512)
    for start in range(0, rows, step):
        index = lax.broadcasted_iota(jnp.int32, (LANES, step), 0)
        hot = of_line[:, start:start + step]
        value = sum(dot(p, hot) for p in pieces)
        out[:, start:start + step] = jnp.sum(
            jnp.where(index == low[:, start:start + step], value, 0.0), axis=0, keepdims=True)


def spare_kernel(peers, cap, emb, owner, cluster, out, send, recv, ids_out, ids_in, id_col, row_best, col_best,
                 ret_out, ret_in, slots, table, row_send, row_recv, id_send, id_recv, ret_send, ret_recv):
    me = lax.axis_index("wide")
    rows = emb.shape[0]
    half = peers // 2

    def partner(block):
        hop = block // 2 + (block % 2) * half
        result, bit = 0, 1
        while bit < peers:
            result = result + bit * ((me // bit + hop // bit) % 2)
            bit *= 2
        return result

    def copies(block):
        to = {"wide": partner(block)}
        return (
            pltpu.make_async_remote_copy(
                src_ref=send.at[block], dst_ref=recv.at[block],
                send_sem=row_send.at[block], recv_sem=row_recv.at[block],
                device_id=to, device_id_type=pl.DeviceIdType.MESH),
            pltpu.make_async_remote_copy(
                src_ref=ids_out.at[block], dst_ref=ids_in.at[block],
                send_sem=id_send.at[block], recv_sem=id_recv.at[block],
                device_id=to, device_id_type=pl.DeviceIdType.MESH),
        )

    def answer(block):
        return pltpu.make_async_remote_copy(
            src_ref=ret_out.at[block], dst_ref=ret_in.at[block],
            send_sem=ret_send.at[block], recv_sem=ret_recv.at[block],
            device_id={"wide": partner(block)}, device_id_type=pl.DeviceIdType.MESH)

    barrier = pltpu.get_barrier_semaphore()

    @pl.loop(1, peers)
    def _(block):
        pl.semaphore_signal(
            barrier, inc=1, device_id={"wide": partner(block)},
            device_id_type=pl.DeviceIdType.MESH)

    device = owner[...]
    names_of = cluster[...] + 1

    hop = jnp.bitwise_xor(device, me)
    block_of = jnp.where(hop >= half, 2 * hop - peers + 1, 2 * hop)
    upto = (
        lax.broadcasted_iota(jnp.int32, (LANES, LANES), 0)
        <= lax.broadcasted_iota(jnp.int32, (LANES, LANES), 1)
    ).astype(jnp.float32).astype(jnp.bfloat16)
    seen = jnp.zeros((peers, 1), jnp.float32)
    for start in range(0, rows, LANES):
        part = block_of[:, start:start + LANES]
        hot = (lax.broadcasted_iota(jnp.int32, (peers, LANES), 0) == part).astype(jnp.float32)
        count = jnp.dot(hot.astype(jnp.bfloat16), upto, preferred_element_type=jnp.float32)
        rank = jnp.sum(hot * (count + seen), axis=0, keepdims=True) - 1.0
        slots[:, start:start + LANES] = part * cap + rank.astype(jnp.int32)
        seen = seen + count[:, LANES - 1:LANES]

    def pack(block, row_ref, id_ref):
        key = slots[...] - block * cap
        hot = (lax.broadcasted_iota(jnp.int32, (cap, rows), 0) == key).astype(jnp.float32)
        hot = hot.astype(jnp.bfloat16)
        picked = jnp.dot(hot, emb[...], preferred_element_type=jnp.float32)
        scale = lax.rsqrt(jnp.sum(picked * picked, axis=1, keepdims=True) + 1e-06)
        row_ref[block] = (picked * scale).astype(jnp.bfloat16)
        label = jnp.broadcast_to(names_of.astype(jnp.float32), (8, rows))
        id_ref[block] = lax.dot_general(
            label.astype(jnp.bfloat16), hot, (((1,), (1,)), ((), ())),
            preferred_element_type=jnp.float32)

    pl.semaphore_wait(barrier, peers - 1)

    @pl.loop(1, peers)
    def _(block):
        pack(block, send, ids_out)

        @pl.when(block <= WINDOW)
        def _():
            for copy in copies(block):
                copy.start()

    pack(0, recv, ids_in)

    def score(new):
        label = ids_in[new][0:1, :]
        id_col[new] = jnp.broadcast_to(label, (LANES, cap)).T
        row_best[new] = jnp.full((cap, LANES), -1.0, jnp.float32)
        rhs = recv[new]
        tile = lax.dot_general(
            rhs, rhs, (((1,), (1,)), ((), ())), preferred_element_type=jnp.float32)
        first = []
        for at in range(0, cap, LANES):
            left = lax.broadcasted_iota(jnp.int32, (cap, LANES), 0)
            right = lax.broadcasted_iota(jnp.int32, (cap, LANES), 1) + at
            same = (id_col[new] == label[:, at:at + LANES]) & (left != right)
            first.append(fold_rows(jnp.where(same, tile[:, at:at + LANES], -1.0)))

        def pair(old):
            tile = lax.dot_general(
                recv[old], recv[new], (((1,), (1,)), ((), ())),
                preferred_element_type=jnp.float32)
            ids = id_col[old]
            run = row_best[old]
            result = []
            for at in range(0, cap, LANES):
                kept = jnp.where(ids == label[:, at:at + LANES], tile[:, at:at + LANES], -1.0)
                run = jnp.maximum(run, kept)
                result.append(fold_rows(kept))
            row_best[old] = run
            return jnp.concatenate(result, axis=1)

        def pairs(step, best):
            return jnp.maximum(best, jnp.maximum(pair(2 * step), pair(2 * step + 1)))

        col_best[new] = lax.fori_loop(0, new // 2, pairs, jnp.concatenate(first, axis=1))

        @pl.when(new % 2 == 1)
        def _():
            col_best[new] = jnp.maximum(col_best[new], pair(new - 1))

    score(0)

    @pl.loop(1, peers)
    def _(block):
        for copy in copies(block):
            copy.wait()

        @pl.when(block + WINDOW < peers)
        def _():
            for copy in copies(block + WINDOW):
                copy.start()

        score(block)

    def total(block):
        return jnp.maximum(col_best[block], fold_rows(row_best[block].T))

    @pl.loop(1, peers)
    def _(block):
        ret_out[block] = total(block)
        answer(block).start()

    ret_in[0] = total(0)
    table[...] = jnp.zeros((LANES, LANES), jnp.float32)

    @pl.loop(1, peers)
    def _(block):
        answer(block).wait()

    each = cap // LANES
    for block in range(peers):
        best = jnp.max(ret_in[block], axis=0, keepdims=True)
        for piece in range(each):
            table[block * each + piece:block * each + piece + 1, :] = (
                best[:, piece * LANES:(piece + 1) * LANES])
    rest = table[...].T
    pieces = []
    for _ in range(3):
        pieces.append(rest.astype(jnp.bfloat16))
        rest = rest - pieces[-1].astype(jnp.float32)
    step = min(rows, 512)
    for start in range(0, rows, step):
        slot = slots[:, start:start + step]
        high = jnp.right_shift(slot, 7)
        low = jnp.bitwise_and(slot, LANES - 1)
        index = lax.broadcasted_iota(jnp.int32, (LANES, step), 0)
        hot = (index == high).astype(jnp.float32).astype(jnp.bfloat16)
        value = sum(jnp.dot(p, hot, preferred_element_type=jnp.float32) for p in pieces)
        out[:, start:start + step] = jnp.sum(
            jnp.where(index == low, value, 0.0), axis=0, keepdims=True)


def solution(mesh):
    peers, groups = mesh.shape["wide"], mesh.shape["groups"]
    vmem = pl.BlockSpec(memory_space=pltpu.VMEM)

    def spare_call(embeddings, owner, cluster):
        rows, width = embeddings.shape
        cap = 2 * rows // peers
        return pl.pallas_call(
            functools.partial(spare_kernel, peers, cap),
            out_shape=jax.ShapeDtypeStruct((1, rows), jnp.float32),
            in_specs=[vmem] * 3,
            out_specs=vmem,
            scratch_shapes=[
                pltpu.VMEM((peers, cap, width), jnp.bfloat16),
                pltpu.VMEM((peers, cap, width), jnp.bfloat16),
                pltpu.VMEM((peers, 8, cap), jnp.float32),
                pltpu.VMEM((peers, 8, cap), jnp.float32),
                pltpu.VMEM((peers, cap, LANES), jnp.float32),
                pltpu.VMEM((peers, cap, LANES), jnp.float32),
                pltpu.VMEM((peers, 8, cap), jnp.float32),
                pltpu.VMEM((peers, 8, cap), jnp.float32),
                pltpu.VMEM((peers, 8, cap), jnp.float32),
                pltpu.VMEM((1, rows), jnp.int32),
                pltpu.VMEM((LANES, LANES), jnp.float32),
            ] + [pltpu.SemaphoreType.DMA((peers,))] * 6,
            compiler_params=pltpu.CompilerParams(
                collective_id=1, has_side_effects=True, vmem_limit_bytes=56 << 20),
        )(embeddings, owner, cluster)

    def call(embeddings, owner, cluster):
        rows, width = embeddings.shape
        near, far, first = sizes_of(rows, peers)
        half = peers // 2
        total = half * (near + far)
        lines = (total // LANES + 8) // 8 * 8
        kinds = 8 * peers
        return pl.pallas_call(
            functools.partial(kernel, peers, groups, near, far, first),
            out_shape=[
                jax.ShapeDtypeStruct((1, rows), jnp.float32),
                jax.ShapeDtypeStruct((1, 1), jnp.int32),
            ],
            in_specs=[pl.BlockSpec(memory_space=pltpu.HBM), vmem, vmem],
            out_specs=[vmem, pl.BlockSpec(memory_space=pltpu.SMEM)],
            scratch_shapes=[
                pltpu.VMEM((rows, width), jnp.bfloat16),
                pltpu.SemaphoreType.DMA(()),
                pltpu.VMEM((LANES, rows), jnp.bfloat16),
                pltpu.VMEM((total, width), jnp.bfloat16),
                pltpu.VMEM((total, width), jnp.bfloat16),
                pltpu.VMEM((total, LANES), jnp.float32),
                pltpu.VMEM((8, total), jnp.float32),
                pltpu.VMEM((total, LANES), jnp.float32),
                pltpu.VMEM((8, total), jnp.float32),
                pltpu.VMEM((lines, LANES), jnp.float32),
                pltpu.VMEM((peers, 8, LANES), jnp.float32),
                pltpu.VMEM((peers, 8, LANES), jnp.float32),
                pltpu.VMEM((kinds, rows), jnp.bfloat16),
                pltpu.VMEM((1, rows), jnp.int32),
                pltpu.VMEM((1, rows), jnp.int32),
                pltpu.VMEM((1, rows), jnp.int32),
                pltpu.VMEM((LANES, LANES), jnp.float32),
                pltpu.VMEM((peers, kinds), jnp.float32),
                pltpu.VMEM((peers, kinds), jnp.float32),
                pltpu.VMEM((8, kinds), jnp.float32),
                pltpu.VMEM((peers, 8, kinds), jnp.float32),
                pltpu.VMEM((peers, kinds), jnp.float32),
                pltpu.VMEM((kinds, peers, LANES), jnp.float32),
                pltpu.VMEM((kinds, LANES), jnp.float32),
                pltpu.VMEM((8, LANES), jnp.float32),
                pltpu.VMEM((groups, 8, LANES), jnp.float32),
            ] + [pltpu.SemaphoreType.DMA((half,))] * 6
            + [pltpu.SemaphoreType.DMA((peers,))] * 4
            + [pltpu.SemaphoreType.DMA((groups,))] * 2,
            compiler_params=pltpu.CompilerParams(
                collective_id=0, has_side_effects=True, vmem_limit_bytes=56 << 20),
        )(embeddings, owner, cluster)

    def per_device(embeddings, row_owner, row_cluster):
        rows = embeddings.shape[0]
        args = (embeddings, row_owner.reshape(1, rows), row_cluster.reshape(1, rows))
        best, over = call(*args)
        best = lax.cond(over[0, 0] > 0, lambda: spare_call(*args), lambda: best)
        return best.reshape(rows)

    return jax.shard_map(
        per_device,
        mesh=mesh,
        in_specs=(P(("groups", "wide"), None), P(("groups", "wide"), None), P(("groups", "wide"))),
        out_specs=P(("groups", "wide")),
        check_vma=False,
    )
```
